32 devices in a mesh: plane: 4 (over y, core), frame: 8 (over z, x).
Axes of the slice: x: 2, y: 2, z: 4, core: 2. Of those that a mesh axis runs over, the one named last changes fastest.
Arguments:
- image: float32 [8, 8, 2, 128, 128], P('plane', 'frame'), may hold values from -6 to 6
- sens: bfloat16 [4, 8, 2, 128, 128], P(None, 'plane'), may hold values from -3 to 3
- kspace: bfloat16 [4, 8, 8, 2, 128, 128], P(None, 'plane', 'frame'), may hold values from -6 to 6
- offsets: int32 [8, 128], P('frame'), may hold values from 0 to 3
- shifts: int32 [2], replicated, may hold values from 0 to 7
- step_size: float32 [1], replicated, may hold values from 0.5 to 1.5
- threshold: float32 [1], replicated, may hold values from 100 to 1000
Outputs:
- new_image: float32 [8, 8, 2, 128, 128], P('plane', 'frame')
The draws below stay inside these ranges and needn't reach their ends.
All inputs are finite; a program needn't handle non-finite values.
Results may differ from the reference program's by a relative error of at most 0.0003.
Values sent between devices are 32-bit elements; how exact they have to be, the bound alone decides.
A program may use at most 64 MiB of HBM per device.

```python
import math
import jax
import jax.numpy as jnp
from jax import lax

NY = 128
NZ = 128
COILS = 4
PATCH_X = 4
PATCH_Y = 8
PATCH_Z = 8
ACCEL = 4
CENTER = 8
NX = 8
FRAMES = 8


def touch_ends(values, stream_key, low, top_value):
    dims = values.shape
    spot = [jax.random.randint(jax.random.fold_in(stream_key, axis), (), 0, dims[axis]) for axis in range(len(dims))]
    values = values.at[tuple(spot)].set(low)
    longest = dims.index(max(dims))
    spot[longest] = (spot[longest] + 1) % dims[longest]
    return values.at[tuple(spot)].set(top_value)


def block_scale(stream_key, extent, cuts, low, high):
    loudness, own = 1.0, jax.random.fold_in(stream_key, 6)
    for axis_at, blocks in cuts:
        draws = jnp.exp(jax.random.uniform(jax.random.fold_in(own, axis_at), (blocks,), jnp.float32, low / len(cuts), high / len(cuts)))
        loudness = loudness * jnp.repeat(draws, extent[axis_at] // blocks).reshape([-1 if axis == axis_at else 1 for axis in range(len(extent))])
    return loudness


def bell_draw(stream_key, shape, deviation, most, split=(), held_as=jnp.bfloat16):
    values = deviation * jax.random.normal(stream_key, shape, jnp.float32)
    if split:
        values = values * block_scale(stream_key, shape, split, -0.22, 0.18)
    return jnp.clip(values, -most, most).astype(held_as)


def setup_inputs(seed: int = 0) -> dict:
    key_list = jax.random.split(jax.random.key(seed), 8)
    return {
        "image": bell_draw(key_list[0], (NX, FRAMES, 2, NY, NZ), 1.0, 6.0, ((0, 4), (1, 8)), jnp.float32),
        "sens": bell_draw(key_list[1], (COILS, NX, 2, NY, NZ), 0.5, 3.0, ((1, 4),)),
        "kspace": bell_draw(key_list[2], (COILS, NX, FRAMES, 2, NY, NZ), 1.0, 6.0, ((1, 4), (2, 8))),
        "offsets": touch_ends(jax.random.randint(key_list[3], (FRAMES, NY), 0, ACCEL), jax.random.fold_in(key_list[3], 1), 0, ACCEL - 1).astype(jnp.int32),
        "shifts": jax.random.randint(key_list[4], (2,), 0, PATCH_Y).astype(jnp.int32),
        "step_size": jnp.clip(jax.random.uniform(key_list[5], (1,), jnp.float32, 0.5, 1.5), 0.5, 1.5),
        "threshold": jnp.clip(jnp.exp(jax.random.uniform(key_list[6], (1,), jnp.float32, math.log(100.0), math.log(1000.0))), 100.0, 1000.0),
    }


def rotate(casorati):
    frames2, voxels = (casorati.shape[-2], casorati.shape[-1])
    split_parts = casorati.reshape(casorati.shape[:-2] + (frames2 // 2, 2, voxels))
    turned = jnp.stack([-split_parts[..., 1, :], split_parts[..., 0, :]], axis=-2)
    return turned.reshape(casorati.shape)

def gram_of(casorati):
    twin = rotate(casorati)
    first = jnp.einsum('...av,...bv->...ab', casorati.astype(jnp.float32), casorati.astype(jnp.float32), precision=lax.Precision.HIGHEST, preferred_element_type=jnp.float32)
    second = jnp.einsum('...av,...bv->...ab', twin.astype(jnp.float32), twin.astype(jnp.float32), precision=lax.Precision.HIGHEST, preferred_element_type=jnp.float32)
    return first + second

def shrink(casorati, gram, level):
    order = gram.shape[-1]
    system = gram + level * jnp.eye(order, dtype=jnp.float32)
    factor = jnp.linalg.cholesky(system)
    forward_part = jax.scipy.linalg.solve_triangular(factor, casorati, lower=True)
    solved = jax.scipy.linalg.solve_triangular(factor, forward_part, lower=True, trans=1)
    return casorati - level * solved

def reference(image, sens, kspace, offsets, shifts, step_size, threshold):
    rows_y = jnp.arange(NY, dtype=jnp.int32)
    rows_z = jnp.arange(NZ, dtype=jnp.int32)
    low_y = (rows_y < CENTER) | (rows_y >= NY - CENTER)
    low_z = (rows_z < CENTER) | (rows_z >= NZ - CENTER)
    regular = (rows_z[None, None, :] + offsets[:, :, None]) % ACCEL == 0
    sampled = (regular | low_y[None, :, None] & low_z[None, None, :]).astype(jnp.float32)
    step = step_size[0]

    def plane_step(inputs):
        plane_img, plane_sens, plane_data = inputs
        xc = plane_img[:, 0] + 1j * plane_img[:, 1]
        coil_maps = plane_sens[:, 0].astype(jnp.float32) + 1j * plane_sens[:, 1].astype(jnp.float32)
        measured = plane_data[:, :, 0].astype(jnp.float32) + 1j * plane_data[:, :, 1].astype(jnp.float32)
        coil_images = coil_maps[:, None] * xc[None]
        spectra = jnp.fft.fft2(coil_images, norm='ortho')
        resid = sampled[None] * (spectra - measured)
        returned = jnp.fft.ifft2(resid, norm='ortho')
        grad = jnp.sum(jnp.conj(coil_maps)[:, None] * returned, axis=0)
        return plane_img - step * jnp.stack([grad.real, grad.imag], axis=1)
    moved = lax.map(plane_step, (image, jnp.moveaxis(sens, 1, 0), jnp.moveaxis(kspace, 1, 0)))
    rolled = jnp.roll(moved, (shifts[0], shifts[1]), axis=(3, 4))
    nxb, nyb, nzb = (NX // PATCH_X, NY // PATCH_Y, NZ // PATCH_Z)
    pieces = rolled.reshape(nxb, PATCH_X, FRAMES, 2, nyb, PATCH_Y, nzb, PATCH_Z)
    pieces = pieces.transpose(0, 4, 6, 2, 3, 1, 5, 7).reshape(nxb * nyb * nzb, 2 * FRAMES, PATCH_X * PATCH_Y * PATCH_Z)
    level = threshold[0]

    def one_patch(casorati):
        return shrink(casorati, gram_of(casorati), level)
    shrunk = lax.map(one_patch, pieces)
    placed = shrunk.reshape(nxb, nyb, nzb, FRAMES, 2, PATCH_X, PATCH_Y, PATCH_Z)
    placed = placed.transpose(0, 5, 3, 4, 1, 6, 2, 7).reshape(NX, FRAMES, 2, NY, NZ)
    return jnp.roll(placed, (-shifts[0], -shifts[1]), axis=(3, 4))
```

```python
import functools
import math

import jax
import jax.numpy as jnp
import numpy as np
from jax import lax
from jax.experimental import pallas as pl
from jax.experimental.pallas import tpu as pltpu
from jax.sharding import PartitionSpec as P

PATCH_X = 4
PATCH_Y = 8
PATCH_Z = 8
ACCEL = 4
CENTER = 8


def from_partner(block, axis, distance):
    count = lax.axis_size(axis)
    route = []
    for low in range(count):
        high = low | 1 << distance
        if high != low and high < count:
            route += [(low, high), (high, low)]
    return lax.ppermute(block, axis, route)


def dft_tables(length):
    indices = jnp.arange(length, dtype=jnp.int32)
    phases = indices[:, None] * indices[None, :] % length
    angles = phases.astype(jnp.float32) * (2.0 * math.pi / length)
    norm_scale = 1.0 / math.sqrt(length)
    return (jnp.cos(angles) * norm_scale, jnp.sin(angles) * norm_scale)


def along_z(stacked, right_table, sign, width_z):
    product = jnp.einsum(
        "...z,zw->...w",
        stacked,
        right_table,
        precision=lax.Precision.HIGHEST,
        preferred_element_type=jnp.float32,
    )
    cos_part = product[..., :width_z]
    sin_part = product[..., width_z:]
    real_part = cos_part[..., 0, :, :] + sign * sin_part[..., 1, :, :]
    imag_part = cos_part[..., 1, :, :] - sign * sin_part[..., 0, :, :]
    return jnp.stack([real_part, imag_part], axis=-3)


def along_y(stacked, left_table):
    shape_in = stacked.shape
    merged = stacked.reshape(shape_in[:-3] + (2 * shape_in[-2], shape_in[-1]))
    result = jnp.einsum(
        "ur,...rz->...uz",
        left_table,
        merged,
        precision=lax.Precision.HIGHEST,
        preferred_element_type=jnp.float32,
    )
    return result.reshape(shape_in)


def rotate(casorati):
    frames2, voxels = (casorati.shape[-2], casorati.shape[-1])
    split_parts = casorati.reshape(casorati.shape[:-2] + (frames2 // 2, 2, voxels))
    turned = jnp.stack([-split_parts[..., 1, :], split_parts[..., 0, :]], axis=-2)
    return turned.reshape(casorati.shape)


def gram_of(casorati):
    twin = rotate(casorati)
    first = jnp.einsum(
        "kav,kbv->kab",
        casorati,
        casorati,
        precision=lax.Precision.HIGHEST,
        preferred_element_type=jnp.float32,
    )
    second = jnp.einsum(
        "kav,kbv->kab",
        twin,
        twin,
        precision=lax.Precision.HIGHEST,
        preferred_element_type=jnp.float32,
    )
    return first + second


def shrink(casorati, gram, level):
    order = gram.shape[-1]
    system = gram + level * jnp.eye(order, dtype=jnp.float32)
    factor = jnp.linalg.cholesky(system)
    forward_part = jax.scipy.linalg.solve_triangular(factor, casorati, lower=True)
    solved = jax.scipy.linalg.solve_triangular(factor, forward_part, lower=True, trans=1)
    return casorati - level * solved


def local_general(image, sens, kspace, offsets, shifts, step_size, threshold):
    planes, frames_dev, _, width_y, width_z = image.shape
    frames = frames_dev * lax.axis_size("frame")
    cos_y, sin_y = dft_tables(width_y)
    cos_z, sin_z = dft_tables(width_z)
    right_table = jnp.concatenate([cos_z, sin_z], axis=1)
    left_forward = jnp.concatenate(
        [jnp.concatenate([cos_y, sin_y], axis=1), jnp.concatenate([-sin_y, cos_y], axis=1)], axis=0
    )
    left_inverse = jnp.concatenate(
        [jnp.concatenate([cos_y, -sin_y], axis=1), jnp.concatenate([sin_y, cos_y], axis=1)], axis=0
    )
    rows_y = jnp.arange(width_y, dtype=jnp.int32)
    rows_z = jnp.arange(width_z, dtype=jnp.int32)
    low_y = (rows_y < CENTER) | (rows_y >= width_y - CENTER)
    low_z = (rows_z < CENTER) | (rows_z >= width_z - CENTER)
    regular = (rows_z[None, None, :] + offsets[:, :, None]) % ACCEL == 0
    sampled = (regular | low_y[None, :, None] & low_z[None, None, :]).astype(jnp.float32)
    image_re = image[:, :, 0]
    image_im = image[:, :, 1]
    maps = sens.astype(jnp.float32)
    sens_re = maps[:, :, 0][:, :, None]
    sens_im = maps[:, :, 1][:, :, None]
    coil_re = sens_re * image_re[None] - sens_im * image_im[None]
    coil_im = sens_re * image_im[None] + sens_im * image_re[None]
    stacked = jnp.stack([coil_re, coil_im], axis=3)
    spectra = along_y(along_z(stacked, right_table, 1.0, width_z), left_forward)
    resid = sampled[None, None, :, None] * (spectra - kspace.astype(jnp.float32))
    returned = along_z(along_y(resid, left_inverse), right_table, -1.0, width_z)
    back_re = returned[:, :, :, 0]
    back_im = returned[:, :, :, 1]
    grad_re = jnp.sum(sens_re * back_re + sens_im * back_im, axis=0)
    grad_im = jnp.sum(sens_re * back_im - sens_im * back_re, axis=0)
    moved = image - step_size[0] * jnp.stack([grad_re, grad_im], axis=2)
    rolled = jnp.roll(moved, (shifts[0], shifts[1]), axis=(3, 4))
    nyb = width_y // PATCH_Y
    nzb = width_z // PATCH_Z
    voxels = planes * PATCH_Y * PATCH_Z
    blocks = rolled.reshape(planes, frames_dev, 2, nyb, PATCH_Y, nzb, PATCH_Z)
    blocks = blocks.transpose(3, 5, 1, 2, 0, 4, 6).reshape(nyb * nzb, frames_dev, 2, voxels)
    regrouped = lax.all_to_all(blocks, "frame", split_axis=0, concat_axis=1, tiled=True)
    count = regrouped.shape[0]
    casorati = regrouped.reshape(count, 2 * frames, voxels)
    level = threshold[0]
    parity = lax.axis_index("plane") % 2
    halfway = count // 2
    first_part = casorati[:halfway]
    second_part = casorati[halfway:]
    kept_part = jnp.where(parity == 0, first_part, second_part)
    outgoing = jnp.where(parity == 0, second_part, first_part)
    incoming = from_partner(outgoing, "plane", 0)
    complete = jnp.concatenate([kept_part, incoming], axis=2)
    finished = shrink(complete, gram_of(complete), level)
    own_part = finished[:, :, :voxels]
    returned_part = from_partner(finished[:, :, voxels:], "plane", 0)
    shrunk = jnp.where(
        parity == 0,
        jnp.concatenate([own_part, returned_part], axis=0),
        jnp.concatenate([returned_part, own_part], axis=0),
    )
    restored = lax.all_to_all(
        shrunk.reshape(count, frames, 2, voxels), "frame", split_axis=1, concat_axis=0, tiled=True
    )
    placed = restored.reshape(nyb, nzb, frames_dev, 2, planes, PATCH_Y, PATCH_Z)
    placed = placed.transpose(4, 2, 3, 0, 5, 1, 6).reshape(planes, frames_dev, 2, width_y, width_z)
    return jnp.roll(placed, (-shifts[0], -shifts[1]), axis=(3, 4))


VMEM_BYTES = 24 * 1024 * 1024


def block_tables(length):
    indices = np.arange(length)
    angles = (indices[:, None] * indices[None, :] % length) * (2.0 * np.pi / length)
    cos = np.cos(angles) / np.sqrt(length)
    sin = np.sin(angles) / np.sqrt(length)
    parts = []
    for table in (cos, sin):
        high = table.astype(jnp.bfloat16)
        parts += [high, (table - high.astype(np.float64)).astype(jnp.bfloat16)]
    return np.stack(parts)


def lay_tables(parts_ref, table_ref, width):
    low, top = pl.ds(0, width), pl.ds(width, width)
    for k in range(2):
        cos, sin = parts_ref[k], parts_ref[2 + k]
        for table, upper, lower in ((k, sin, -sin), (2 + k, -sin, sin)):
            table_ref[table, low, low] = cos
            table_ref[table, top, top] = cos
            table_ref[table, low, top] = upper
            table_ref[table, top, low] = lower


def halves(values):
    high = values.astype(jnp.bfloat16)
    return high, (values - high.astype(jnp.float32)).astype(jnp.bfloat16)


def mul(left, right):
    return jnp.dot(left, right, preferred_element_type=jnp.float32)


def from_right(values, high, low):
    value_high, value_low = halves(values)
    return mul(value_high, high) + mul(value_high, low) + mul(value_low, high)


def from_left(high, low, values):
    value_high, value_low = halves(values)
    return mul(high, value_high) + mul(low, value_high) + mul(high, value_low)


def rows_to_lanes(values, coils, width):
    parts = [
        jnp.concatenate([values[c * width : (c + 1) * width, k * width : (k + 1) * width] for c in range(coils)], axis=1)
        for k in range(2)
    ]
    return jnp.concatenate(parts, axis=0)


def lanes_to_rows(values, coils, width):
    parts = [
        jnp.concatenate([values[k * width : (k + 1) * width, c * width : (c + 1) * width] for k in range(2)], axis=1)
        for c in range(coils)
    ]
    return jnp.concatenate(parts, axis=0)


def moved_plane(loads, start_later, p, coils, width, image_ref, sens_ref, kspace_ref, table_ref, step, sampled):
    loads["image", p].wait()
    loads["sens", p].wait()
    image_re = image_ref[p, 0, 0]
    image_im = image_ref[p, 0, 1]
    stacked = []
    for c in range(coils):
        sens_re = sens_ref[c, p, 0].astype(jnp.float32)
        sens_im = sens_ref[c, p, 1].astype(jnp.float32)
        stacked.append(
            jnp.concatenate(
                [sens_re * image_re - sens_im * image_im, sens_re * image_im + sens_im * image_re], axis=1
            )
        )
    along = from_right(jnp.concatenate(stacked, axis=0), table_ref[2], table_ref[3])
    spectra = from_left(table_ref[0], table_ref[1], rows_to_lanes(along, coils, width))
    loads["kspace", p].wait()
    if p == 0:
        start_later()
    data = jnp.concatenate(
        [
            jnp.concatenate([kspace_ref[c, p, 0, k].astype(jnp.float32) for c in range(coils)], axis=1)
            for k in range(2)
        ],
        axis=0,
    )
    weight = jnp.concatenate([jnp.concatenate([sampled] * coils, axis=1)] * 2, axis=0)
    resid = weight * (spectra - data)
    back = from_left(table_ref[2], table_ref[3], resid)
    returned = from_right(lanes_to_rows(back, coils, width), table_ref[0], table_ref[1])
    grad_re = jnp.zeros_like(image_re)
    grad_im = jnp.zeros_like(image_im)
    for c in range(coils):
        back_re = returned[c * width : (c + 1) * width, :width]
        back_im = returned[c * width : (c + 1) * width, width:]
        sens_re = sens_ref[c, p, 0].astype(jnp.float32)
        sens_im = sens_ref[c, p, 1].astype(jnp.float32)
        grad_re += sens_re * back_re + sens_im * back_im
        grad_im += sens_re * back_im - sens_im * back_re
    return image_re - step * grad_re, image_im - step * grad_im


def sweep(matrix, order):
    for k in range(order):
        pivot = 1.0 / matrix[k, k][0]
        column = {}
        for i in range(order):
            if i > k:
                column[i] = matrix[i, k]
            elif i < k:
                column[i] = (matrix[k, i][0], -matrix[k, i][1])
        scaled = {i: (re * pivot, im * pivot) for i, (re, im) in column.items()}
        for i in column:
            for j in column:
                if j > i:
                    continue
                a_re, a_im = scaled[i]
                b_re, b_im = column[j]
                re, im = matrix[i, j]
                re = re - (a_re * b_re + a_im * b_im)
                if i != j:
                    im = im - (a_im * b_re - a_re * b_im)
                matrix[i, j] = (re, im)
        for i in column:
            if i > k:
                matrix[i, k] = scaled[i]
            else:
                matrix[k, i] = (scaled[i][0], -scaled[i][1])
        matrix[k, k] = (-pivot, None)
    return matrix


def step_kernel(
    planes, frames, group, coils, width_y, width_z,
    shifts_ref, step_ref, level_ref, offsets_ref, image_hbm, sens_hbm, kspace_hbm, table_hbm,
    landed,
    image_ref, sens_ref, kspace_ref, parts_ref, table_ref, load_sem,
    wrapped, rolled, gathered, entries, inverse, finished,
    send_out, recv_out, send_back, recv_back, own_out, own_back,
):
    total = frames * group
    plane_me = lax.axis_index("plane")
    frame_me = lax.axis_index("frame")
    part_me = lax.rem(plane_me, group)
    base = plane_me - part_me
    me = frame_me * group + part_me
    rows = PATCH_Y

    def flip(index, mask, count):
        bit = 1
        while bit < count:
            if mask & bit:
                index = index + bit - 2 * bit * lax.rem(index // bit, 2)
            bit *= 2
        return index

    def device(index):
        return {"plane": base + lax.rem(index, group), "frame": index // group}

    loads = {}

    def load(name, source, target):
        loads[name] = pltpu.make_async_copy(source, target, load_sem.at[len(loads)])
        loads[name].start()

    def load_plane(p):
        load(("image", p), image_hbm.at[p], image_ref.at[p])
        load(("sens", p), sens_hbm.at[:, p], sens_ref.at[:, p])
        load(("kspace", p), kspace_hbm.at[:, p], kspace_ref.at[:, p])

    def start_later():
        for p in range(1, planes):
            load_plane(p)

    load("table", table_hbm, parts_ref)
    load_plane(0)

    barrier = pltpu.get_barrier_semaphore()
    for k in range(1, total):
        pl.semaphore_signal(barrier, inc=1, device_id=device(flip(me, k, total)), device_id_type=pl.DeviceIdType.MESH)

    lane = lax.broadcasted_iota(jnp.int32, (width_y, width_z), 1)
    row = lax.broadcasted_iota(jnp.int32, (width_y, width_z), 0)
    offset = jnp.broadcast_to(offsets_ref[...].astype(jnp.float32), (width_z, width_y)).T
    wanted = jnp.where(offset == 0.0, 0.0, ACCEL - offset)
    regular = lax.rem(lane, ACCEL).astype(jnp.float32) == wanted
    low_y = (row < CENTER) | (row >= width_y - CENTER)
    low_z = (lane < CENTER) | (lane >= width_z - CENTER)
    sampled = (regular | (low_y & low_z)).astype(jnp.float32)

    sends = []
    loads["table"].wait()
    lay_tables(parts_ref, table_ref, width_y)
    for p in range(planes):
        moved = moved_plane(loads, start_later, p, coils, width_y, image_ref, sens_ref, kspace_ref, table_ref, step_ref[0], sampled)
        for k in range(2):
            part = pltpu.roll(moved[k], shifts_ref[1], 1)
            wrapped[p, k, pl.ds(0, rows), :] = part[width_y - rows :]
            wrapped[p, k, pl.ds(rows, width_y), :] = part
            rolled[p, k] = wrapped[p, k, pl.ds(rows - shifts_ref[0], width_y), :]
        if p == 0:
            pl.semaphore_wait(barrier, total - 1)
        group_sends = []
        for k in reversed(range(1, total)):
            target = flip(me, k, total)
            copy = pltpu.make_async_remote_copy(
                src_ref=rolled.at[p, :, pl.ds(pl.multiple_of(target * rows, rows), rows), :],
                dst_ref=gathered.at[p, part_me, frame_me],
                send_sem=send_out.at[p, k],
                recv_sem=recv_out.at[p, k],
                device_id=device(target),
                device_id_type=pl.DeviceIdType.MESH,
            )
            copy.start()
            group_sends.append(copy)
        own = pltpu.make_async_copy(
            rolled.at[p, :, pl.ds(pl.multiple_of(me * rows, rows), rows), :],
            gathered.at[p, part_me, frame_me],
            own_out.at[p],
        )
        own.start()
        sends.append((group_sends, own))

    pairs = [(f, g) for f in range(frames) for g in range(f + 1)]
    for p in range(planes):
        group_sends, own = sends[p]
        own.wait()
        for copy in group_sends:
            copy.wait_recv()
        for n, (f, g) in enumerate(pairs):
            sum_re = None
            sum_im = None
            for q in range(group):
                f_re, f_im = gathered[p, q, f, 0], gathered[p, q, f, 1]
                g_re, g_im = gathered[p, q, g, 0], gathered[p, q, g, 1]
                re = f_re * g_re + f_im * g_im
                sum_re = re if sum_re is None else sum_re + re
                if f != g:
                    im = f_im * g_re - f_re * g_im
                    sum_im = im if sum_im is None else sum_im + im
            spot = f * frames + g
            entries[spot] = sum_re if p == 0 else entries[spot] + sum_re
            if f != g:
                spot = g * frames + f
                entries[spot] = sum_im if p == 0 else entries[spot] + sum_im

    one_row = lax.broadcasted_iota(jnp.int32, (width_z, width_z), 0) // PATCH_Z
    one_lane = lax.broadcasted_iota(jnp.int32, (width_z, width_z), 1) // PATCH_Z
    same = (one_row == one_lane).astype(jnp.bfloat16)
    cells = entries[...]
    shift = rows // 2
    while shift:
        cells = cells + pltpu.roll(cells, shift, 1)
        shift //= 2
    high, low = halves(cells.reshape(frames * frames * rows, width_z))
    entries[...] = (mul(high, same) + mul(low, same)).reshape(frames * frames, rows, width_z)

    level = level_ref[0]
    matrix = {}
    for f, g in pairs:
        if f == g:
            matrix[f, f] = (entries[f * frames + f] + level, None)
        else:
            matrix[f, g] = (entries[f * frames + g], entries[g * frames + f])
    matrix = sweep(matrix, frames)
    for f, g in pairs:
        re, im = matrix[f, g]
        inverse[f, g, 0] = re * level
        if f != g:
            inverse[f, g, 1] = im * level
            inverse[g, f, 0] = re * level
            inverse[g, f, 1] = -im * level
        else:
            inverse[f, f, 1] = jnp.zeros_like(re)

    backs = []
    spot = pl.ds(pl.multiple_of(me * rows, rows), rows)
    for f in range(frames):
        weights = [(inverse[f, g, 0], inverse[f, g, 1]) for g in range(frames)]
        for q in range(group):
            for p in range(planes):
                re = gathered[p, q, f, 0]
                im = gathered[p, q, f, 1]
                for g in range(frames):
                    g_re, g_im = gathered[p, q, g, 0], gathered[p, q, g, 1]
                    w_re, w_im = weights[g]
                    re = re + (w_re * g_re - w_im * g_im)
                    im = im + (w_re * g_im + w_im * g_re)
                finished[q, f, p, 0] = re
                finished[q, f, p, 1] = im
            mine = (frame_me == f) & (part_me == q)
            local = pltpu.make_async_copy(finished.at[q, f], landed.at[:, 0, :, spot, :], own_back)
            copy = pltpu.make_async_remote_copy(
                src_ref=finished.at[q, f],
                dst_ref=landed.at[:, 0, :, spot, :],
                send_sem=send_back.at[q, f],
                recv_sem=recv_back.at[part_me, frame_me],
                device_id={"plane": base + q, "frame": f},
                device_id_type=pl.DeviceIdType.MESH,
            )
            pl.when(mine)(local.start)
            pl.when(jnp.logical_not(mine))(copy.start)
            backs.append((mine, copy))
    local.wait()
    for f in range(frames):
        for q in range(group):
            other = jnp.logical_not((frame_me == f) & (part_me == q))
            copy = pltpu.make_async_remote_copy(
                src_ref=finished.at[q, f],
                dst_ref=landed.at[:, 0, :, pl.ds((f * group + q) * rows, rows), :],
                send_sem=send_back.at[q, f],
                recv_sem=recv_back.at[q, f],
                device_id={"plane": base + q, "frame": f},
                device_id_type=pl.DeviceIdType.MESH,
            )
            pl.when(other)(copy.wait)
    for group_sends, own in sends:
        for copy in group_sends:
            copy.wait_send()


def unroll_kernel(planes, width_y, width_z, shifts_ref, landed_ref, out_ref, wrapped):
    shift_z = lax.rem(width_z - shifts_ref[1], width_z)
    for p in range(planes):
        for k in range(2):
            part = pltpu.roll(landed_ref[p, 0, k], shift_z, 1)
            wrapped[p, k, pl.ds(0, width_y), :] = part
            wrapped[p, k, pl.ds(width_y, PATCH_Y), :] = part[:PATCH_Y]
            out_ref[p, 0, k] = wrapped[p, k, pl.ds(shifts_ref[0], width_y), :]


def local_fused(image, sens, kspace, offsets, shifts, step_size, threshold):
    planes, _, _, width_y, width_z = image.shape
    coils = sens.shape[0]
    frames = lax.axis_size("frame")
    group = PATCH_X // planes
    total = frames * group
    table = jnp.asarray(block_tables(width_y))
    vmem = pl.BlockSpec(memory_space=pltpu.VMEM)
    smem = pl.BlockSpec(memory_space=pltpu.SMEM)
    hbm = pl.BlockSpec(memory_space=pltpu.HBM)
    slab = (PATCH_Y, width_z)
    dma = pltpu.SemaphoreType.DMA
    image, sens, kspace, table = [pltpu.with_memory_space_constraint(x, pltpu.HBM) for x in (image, sens, kspace, table)]
    landed = pl.pallas_call(
        functools.partial(step_kernel, planes, frames, group, coils, width_y, width_z),
        out_shape=jax.ShapeDtypeStruct(image.shape, jnp.float32),
        in_specs=[smem, smem, smem, vmem, hbm, hbm, hbm, hbm],
        out_specs=pl.BlockSpec(memory_space=pl.ANY),
        scratch_shapes=[
            pltpu.VMEM(image.shape, image.dtype),
            pltpu.VMEM(sens.shape, sens.dtype),
            pltpu.VMEM(kspace.shape, kspace.dtype),
            pltpu.VMEM(table.shape, table.dtype),
            pltpu.VMEM((4, 2 * width_y, 2 * width_y), table.dtype),
            dma((3 * planes + 1,)),
            pltpu.VMEM((planes, 2, width_y + PATCH_Y, width_z), jnp.float32),
            pltpu.VMEM((planes, 2, width_y, width_z), jnp.float32),
            pltpu.VMEM((planes, group, frames, 2) + slab, jnp.float32),
            pltpu.VMEM((frames * frames,) + slab, jnp.float32),
            pltpu.VMEM((frames, frames, 2) + slab, jnp.float32),
            pltpu.VMEM((group, frames, planes, 2) + slab, jnp.float32),
            dma((planes, total)),
            dma((planes, total)),
            dma((group, frames)),
            dma((group, frames)),
            dma((planes,)),
            dma(()),
        ],
        compiler_params=pltpu.CompilerParams(collective_id=0, has_side_effects=True, vmem_limit_bytes=VMEM_BYTES),
        name="prox_step",
    )(shifts, step_size, threshold, offsets, image, sens, kspace, table)
    return pl.pallas_call(
        functools.partial(unroll_kernel, planes, width_y, width_z),
        out_shape=jax.ShapeDtypeStruct(image.shape, jnp.float32),
        in_specs=[smem, vmem],
        out_specs=vmem,
        scratch_shapes=[pltpu.VMEM((planes, 2, width_y + PATCH_Y, width_z), jnp.float32)],
        compiler_params=pltpu.CompilerParams(vmem_limit_bytes=VMEM_BYTES),
        name="shift_back",
    )(shifts, landed)


def local(image, sens, kspace, offsets, shifts, step_size, threshold):
    planes, frames_dev, _, width_y, width_z = image.shape
    frames = frames_dev * lax.axis_size("frame")
    group = PATCH_X // planes
    one_block = frames * group * PATCH_Y == width_y and frames_dev == 1 and frames & (frames - 1) == 0
    split = group > 1 and group & (group - 1) == 0 and lax.axis_size("plane") % group == 0
    if one_block and split and width_y == width_z and width_z % 128 == 0:
        return local_fused(image, sens, kspace, offsets, shifts, step_size, threshold)
    return local_general(image, sens, kspace, offsets, shifts, step_size, threshold)


def solution(mesh):
    in_specs = (
        P("plane", "frame", None, None, None),
        P(None, "plane", None, None, None),
        P(None, "plane", "frame", None, None, None),
        P("frame", None),
        P(),
        P(),
        P(),
    )
    out_specs = P("plane", "frame", None, None, None)
    return jax.shard_map(local, mesh=mesh, in_specs=in_specs, out_specs=out_specs, check_vma=False)
```

```python
import functools
import math

import jax
import jax.numpy as jnp
import numpy as np
from jax import lax
from jax.experimental import pallas as pl
from jax.experimental.pallas import tpu as pltpu
from jax.sharding import PartitionSpec as P

PATCH_X = 4
PATCH_Y = 8
PATCH_Z = 8
ACCEL = 4
CENTER = 8


def from_partner(block, axis, distance):
    count = lax.axis_size(axis)
    route = []
    for low in range(count):
        high = low | 1 << distance
        if high != low and high < count:
            route += [(low, high), (high, low)]
    return lax.ppermute(block, axis, route)


def dft_tables(length):
    indices = jnp.arange(length, dtype=jnp.int32)
    phases = indices[:, None] * indices[None, :] % length
    angles = phases.astype(jnp.float32) * (2.0 * math.pi / length)
    norm_scale = 1.0 / math.sqrt(length)
    return (jnp.cos(angles) * norm_scale, jnp.sin(angles) * norm_scale)


def along_z(stacked, right_table, sign, width_z):
    product = jnp.einsum(
        "...z,zw->...w",
        stacked,
        right_table,
        precision=lax.Precision.HIGHEST,
        preferred_element_type=jnp.float32,
    )
    cos_part = product[..., :width_z]
    sin_part = product[..., width_z:]
    real_part = cos_part[..., 0, :, :] + sign * sin_part[..., 1, :, :]
    imag_part = cos_part[..., 1, :, :] - sign * sin_part[..., 0, :, :]
    return jnp.stack([real_part, imag_part], axis=-3)


def along_y(stacked, left_table):
    shape_in = stacked.shape
    merged = stacked.reshape(shape_in[:-3] + (2 * shape_in[-2], shape_in[-1]))
    result = jnp.einsum(
        "ur,...rz->...uz",
        left_table,
        merged,
        precision=lax.Precision.HIGHEST,
        preferred_element_type=jnp.float32,
    )
    return result.reshape(shape_in)


def rotate(casorati):
    frames2, voxels = (casorati.shape[-2], casorati.shape[-1])
    split_parts = casorati.reshape(casorati.shape[:-2] + (frames2 // 2, 2, voxels))
    turned = jnp.stack([-split_parts[..., 1, :], split_parts[..., 0, :]], axis=-2)
    return turned.reshape(casorati.shape)


def gram_of(casorati):
    twin = rotate(casorati)
    first = jnp.einsum(
        "kav,kbv->kab",
        casorati,
        casorati,
        precision=lax.Precision.HIGHEST,
        preferred_element_type=jnp.float32,
    )
    second = jnp.einsum(
        "kav,kbv->kab",
        twin,
        twin,
        precision=lax.Precision.HIGHEST,
        preferred_element_type=jnp.float32,
    )
    return first + second


def shrink(casorati, gram, level):
    order = gram.shape[-1]
    system = gram + level * jnp.eye(order, dtype=jnp.float32)
    factor = jnp.linalg.cholesky(system)
    forward_part = jax.scipy.linalg.solve_triangular(factor, casorati, lower=True)
    solved = jax.scipy.linalg.solve_triangular(factor, forward_part, lower=True, trans=1)
    return casorati - level * solved


def local_general(image, sens, kspace, offsets, shifts, step_size, threshold):
    planes, frames_dev, _, width_y, width_z = image.shape
    frames = frames_dev * lax.axis_size("frame")
    cos_y, sin_y = dft_tables(width_y)
    cos_z, sin_z = dft_tables(width_z)
    right_table = jnp.concatenate([cos_z, sin_z], axis=1)
    left_forward = jnp.concatenate(
        [jnp.concatenate([cos_y, sin_y], axis=1), jnp.concatenate([-sin_y, cos_y], axis=1)], axis=0
    )
    left_inverse = jnp.concatenate(
        [jnp.concatenate([cos_y, -sin_y], axis=1), jnp.concatenate([sin_y, cos_y], axis=1)], axis=0
    )
    rows_y = jnp.arange(width_y, dtype=jnp.int32)
    rows_z = jnp.arange(width_z, dtype=jnp.int32)
    low_y = (rows_y < CENTER) | (rows_y >= width_y - CENTER)
    low_z = (rows_z < CENTER) | (rows_z >= width_z - CENTER)
    regular = (rows_z[None, None, :] + offsets[:, :, None]) % ACCEL == 0
    sampled = (regular | low_y[None, :, None] & low_z[None, None, :]).astype(jnp.float32)
    image_re = image[:, :, 0]
    image_im = image[:, :, 1]
    maps = sens.astype(jnp.float32)
    sens_re = maps[:, :, 0][:, :, None]
    sens_im = maps[:, :, 1][:, :, None]
    coil_re = sens_re * image_re[None] - sens_im * image_im[None]
    coil_im = sens_re * image_im[None] + sens_im * image_re[None]
    stacked = jnp.stack([coil_re, coil_im], axis=3)
    spectra = along_y(along_z(stacked, right_table, 1.0, width_z), left_forward)
    resid = sampled[None, None, :, None] * (spectra - kspace.astype(jnp.float32))
    returned = along_z(along_y(resid, left_inverse), right_table, -1.0, width_z)
    back_re = returned[:, :, :, 0]
    back_im = returned[:, :, :, 1]
    grad_re = jnp.sum(sens_re * back_re + sens_im * back_im, axis=0)
    grad_im = jnp.sum(sens_re * back_im - sens_im * back_re, axis=0)
    moved = image - step_size[0] * jnp.stack([grad_re, grad_im], axis=2)
    rolled = jnp.roll(moved, (shifts[0], shifts[1]), axis=(3, 4))
    nyb = width_y // PATCH_Y
    nzb = width_z // PATCH_Z
    voxels = planes * PATCH_Y * PATCH_Z
    blocks = rolled.reshape(planes, frames_dev, 2, nyb, PATCH_Y, nzb, PATCH_Z)
    blocks = blocks.transpose(3, 5, 1, 2, 0, 4, 6).reshape(nyb * nzb, frames_dev, 2, voxels)
    regrouped = lax.all_to_all(blocks, "frame", split_axis=0, concat_axis=1, tiled=True)
    count = regrouped.shape[0]
    casorati = regrouped.reshape(count, 2 * frames, voxels)
    level = threshold[0]
    parity = lax.axis_index("plane") % 2
    halfway = count // 2
    first_part = casorati[:halfway]
    second_part = casorati[halfway:]
    kept_part = jnp.where(parity == 0, first_part, second_part)
    outgoing = jnp.where(parity == 0, second_part, first_part)
    incoming = from_partner(outgoing, "plane", 0)
    complete = jnp.concatenate([kept_part, incoming], axis=2)
    finished = shrink(complete, gram_of(complete), level)
    own_part = finished[:, :, :voxels]
    returned_part = from_partner(finished[:, :, voxels:], "plane", 0)
    shrunk = jnp.where(
        parity == 0,
        jnp.concatenate([own_part, returned_part], axis=0),
        jnp.concatenate([returned_part, own_part], axis=0),
    )
    restored = lax.all_to_all(
        shrunk.reshape(count, frames, 2, voxels), "frame", split_axis=1, concat_axis=0, tiled=True
    )
    placed = restored.reshape(nyb, nzb, frames_dev, 2, planes, PATCH_Y, PATCH_Z)
    placed = placed.transpose(4, 2, 3, 0, 5, 1, 6).reshape(planes, frames_dev, 2, width_y, width_z)
    return jnp.roll(placed, (-shifts[0], -shifts[1]), axis=(3, 4))


VMEM_BYTES = 24 * 1024 * 1024


ORDERS = ('near', 'near')


def block_tables(length):
    indices = np.arange(length)
    angles = (indices[:, None] * indices[None, :] % length) * (2.0 * np.pi / length)
    cos = np.cos(angles) / np.sqrt(length)
    sin = np.sin(angles) / np.sqrt(length)
    parts = []
    for table in (cos, sin):
        high = table.astype(jnp.bfloat16)
        parts += [high, (table - high.astype(np.float64)).astype(jnp.bfloat16)]
    return np.stack(parts)


def lay_tables(parts_ref, table_ref, width):
    low, top = pl.ds(0, width), pl.ds(width, width)
    for k in range(2):
        cos, sin = parts_ref[k], parts_ref[2 + k]
        for table, upper, lower in ((k, sin, -sin), (2 + k, -sin, sin)):
            table_ref[table, low, low] = cos
            table_ref[table, top, top] = cos
            table_ref[table, low, top] = upper
            table_ref[table, top, low] = lower


def halves(values):
    high = values.astype(jnp.bfloat16)
    return high, (values - high.astype(jnp.float32)).astype(jnp.bfloat16)


def mul(left, right):
    return jnp.dot(left, right, preferred_element_type=jnp.float32)


def from_right(values, high, low):
    value_high, value_low = halves(values)
    return mul(value_high, high) + mul(value_high, low) + mul(value_low, high)


def from_left(high, low, values):
    value_high, value_low = halves(values)
    return mul(high, value_high) + mul(low, value_high) + mul(high, value_low)


def row_patterns(offsets_ref, offset_rows, width_y, width_z):
    lane = lax.broadcasted_iota(jnp.int32, (width_y, width_z), 1)
    row = lax.broadcasted_iota(jnp.int32, (width_y, width_z), 0)
    offset = jnp.broadcast_to(offsets_ref[...].astype(jnp.float32), (width_z, width_y)).T
    wanted = jnp.where(offset == 0.0, 0.0, ACCEL - offset)
    regular = lax.rem(lane, ACCEL).astype(jnp.float32) == wanted
    low_y = (row < CENTER) | (row >= width_y - CENTER)
    low_z = (lane < CENTER) | (lane >= width_z - CENTER)
    centre = low_y & low_z
    scale = float(ACCEL)
    kept = jnp.where(regular | centre, scale, 0.0).astype(jnp.bfloat16)
    extra = jnp.where(centre & jnp.logical_not(regular), scale, 0.0)
    edge = jnp.concatenate([extra[:CENTER], extra[width_y - CENTER :]], axis=0)
    half = jnp.where((offset == 0.0) | (offset == 2.0), 1.0, -1.0)
    real = jnp.where(offset == 0.0, 1.0, jnp.where(offset == 2.0, -1.0, 0.0))
    imag = jnp.where(offset == 1.0, -1.0, jnp.where(offset == 3.0, 1.0, 0.0))
    return kept, edge, half, real, imag


def moved_plane(loads, p, coils, width, image_ref, sens_ref, kspace_ref, table_ref, step, patterns):
    kept, edge, half, real, imag = patterns
    loads["kspace", p].wait()
    data = jnp.concatenate(
        [
            jnp.concatenate([kspace_ref[c, p, 0, k] * kept for k in range(2)], axis=1)
            for c in range(coils)
        ],
        axis=0,
    )
    known = mul(data, table_ref[0]) + mul(data, table_ref[1])
    loads["image", p].wait()
    loads["sens", p].wait()
    image_re = image_ref[p, 0, 0]
    image_im = image_ref[p, 0, 1]
    coil_re, coil_im = [], []
    for c in range(coils):
        sens_re = sens_ref[c, p, 0].astype(jnp.float32)
        sens_im = sens_ref[c, p, 1].astype(jnp.float32)
        coil_re.append(sens_re * image_re - sens_im * image_im)
        coil_im.append(sens_re * image_im + sens_im * image_re)
    stacked = jnp.concatenate([jnp.concatenate(coil_re, axis=1), jnp.concatenate(coil_im, axis=1)], axis=0)
    lines = from_left(table_ref[0], table_ref[1], stacked)

    def part(k, c):
        return lines[k * width : (k + 1) * width, c * width : (c + 1) * width]

    low = jnp.concatenate(
        [
            jnp.concatenate(
                [jnp.concatenate([part(k, c)[:CENTER], part(k, c)[width - CENTER :]], axis=0) for k in range(2)], axis=1
            )
            for c in range(coils)
        ],
        axis=0,
    )
    weight = jnp.concatenate([jnp.concatenate([edge] * 2, axis=1)] * coils, axis=0)
    added = from_right(weight * from_right(low, table_ref[2], table_ref[3]), table_ref[0], table_ref[1])
    resid_re, resid_im = [], []
    for c in range(coils):
        both = []
        for k in range(2):
            line = part(k, c)
            both.append(line + half * pltpu.roll(line, width // 2, 1))
        turned = [pltpu.roll(line, width // 4, 1) for line in both]
        sums = [
            both[0] + (real * turned[0] - imag * turned[1]),
            both[1] + (real * turned[1] + imag * turned[0]),
        ]
        for k, out in ((0, resid_re), (1, resid_im)):
            value = sums[k] - known[c * width : (c + 1) * width, k * width : (k + 1) * width]
            more = added[2 * CENTER * c : 2 * CENTER * (c + 1), k * width : (k + 1) * width]
            out.append(
                jnp.concatenate(
                    [
                        value[:CENTER] + more[:CENTER],
                        value[CENTER : width - CENTER],
                        value[width - CENTER :] + more[CENTER:],
                    ],
                    axis=0,
                )
            )
    resid = jnp.concatenate([jnp.concatenate(resid_re, axis=1), jnp.concatenate(resid_im, axis=1)], axis=0)
    back = from_left(table_ref[2], table_ref[3], resid)
    grad_re = jnp.zeros_like(image_re)
    grad_im = jnp.zeros_like(image_im)
    for c in range(coils):
        back_re = back[:width, c * width : (c + 1) * width]
        back_im = back[width:, c * width : (c + 1) * width]
        sens_re = sens_ref[c, p, 0].astype(jnp.float32)
        sens_im = sens_ref[c, p, 1].astype(jnp.float32)
        grad_re += sens_re * back_re + sens_im * back_im
        grad_im += sens_re * back_im - sens_im * back_re
    scaled = step * (1.0 / ACCEL)
    return image_re - scaled * grad_re, image_im - scaled * grad_im


def sweep(matrix, order):
    for k in range(order):
        pivot = 1.0 / matrix[k, k][0]
        column = {}
        for i in range(order):
            if i > k:
                column[i] = matrix[i, k]
            elif i < k:
                column[i] = (matrix[k, i][0], -matrix[k, i][1])
        scaled = {i: (re * pivot, im * pivot) for i, (re, im) in column.items()}
        for i in column:
            for j in column:
                if j > i:
                    continue
                a_re, a_im = scaled[i]
                b_re, b_im = column[j]
                re, im = matrix[i, j]
                re = re - (a_re * b_re + a_im * b_im)
                if i != j:
                    im = im - (a_im * b_re - a_re * b_im)
                matrix[i, j] = (re, im)
        for i in column:
            if i > k:
                matrix[i, k] = scaled[i]
            else:
                matrix[k, i] = (scaled[i][0], -scaled[i][1])
        matrix[k, k] = (-pivot, None)
    return matrix


def step_kernel(
    planes, frames, group, coils, width_y, width_z,
    step_ref, level_ref, shifts_hbm, offsets_hbm, image_hbm, sens_hbm, kspace_hbm, table_hbm,
    out_ref,
    shifts_ref, offsets_ref, image_ref, sens_ref, kspace_ref, parts_ref, table_ref, load_sem,
    wrapped, rolled, gathered, entries, inverse, finished, landed,
    send_out, recv_out, send_back, recv_back,
):
    total = frames * group
    plane_me = lax.axis_index("plane")
    frame_me = lax.axis_index("frame")
    part_me = lax.rem(plane_me, group)
    base = plane_me - part_me
    me = frame_me * group + part_me
    rows = PATCH_Y
    everyone = [(f, q) for f in range(frames) for q in range(group)]

    def other(f, q):
        return (frame_me != f) | (part_me != q)

    barrier = pltpu.get_barrier_semaphore()
    for f, q in everyone:

        @pl.when(other(f, q))
        def _():
            pl.semaphore_signal(
                barrier, inc=1, device_id={"plane": base + q, "frame": f}, device_id_type=pl.DeviceIdType.MESH
            )

    loads = {}

    def load(name, source, target):
        loads[name] = pltpu.make_async_copy(source, target, load_sem.at[len(loads)])
        loads[name].start()

    load("offsets", offsets_hbm, offsets_ref)
    load("table", table_hbm, parts_ref)
    for p in range(planes):
        load(("kspace", p), kspace_hbm.at[:, p], kspace_ref.at[:, p])
        load(("image", p), image_hbm.at[p], image_ref.at[p])
        load(("sens", p), sens_hbm.at[:, p], sens_ref.at[:, p])
    load("shifts", shifts_hbm, shifts_ref)

    loads["offsets"].wait()
    patterns = row_patterns(offsets_ref, None, width_y, width_z)
    loads["table"].wait()
    lay_tables(parts_ref, table_ref, width_y)

    half, quarter = frames // 2, frames // 4
    far = frame_me // half
    near = 1 - far
    step_in = lax.rem(frame_me // quarter, 2)
    inner = lax.rem(frame_me, quarter)

    def order_out(p):
        if ORDERS[p] == "near":
            pairs_z = [(near, far, False), (far, near, True), (near, near, False), (far, far, True)]
        elif ORDERS[p] == "xor":
            pairs_z = [(near, 1 - step_in, False), (near, step_in, False), (far, 1 - step_in, False), (far, step_in, True)]
        elif ORDERS[p] == "xorn":
            pairs_z = [(near, step_in, False), (near, 1 - step_in, False), (far, 1 - step_in, False), (far, step_in, True)]
        elif ORDERS[p] == "cross":
            pairs_z = [(near, far, False), (near, near, False), (far, near, True), (far, far, True)]
        for z_high, z_low, maybe in pairs_z:
            for k in reversed(range(quarter)):
                x = lax.rem(inner + k, quarter)
                for r in reversed(range(group)):
                    q = lax.rem(part_me + r, group)
                    yield z_high * half + z_low * quarter + x, q, maybe and k == 0 and r == 0

    def send(p, f, q, maybe):
        block = rolled.at[p, :, pl.ds(pl.multiple_of((f * group + q) * rows, rows), rows), :]
        copy = pltpu.make_async_remote_copy(
            src_ref=block,
            dst_ref=gathered.at[p, part_me, frame_me],
            send_sem=send_out.at[p, f, q],
            recv_sem=recv_out.at[p, frame_me, part_me],
            device_id={"plane": base + q, "frame": f},
            device_id_type=pl.DeviceIdType.MESH,
        )
        apart = other(f, q) if maybe else None
        if maybe:
            pl.when(apart)(copy.start)
        else:
            copy.start()
        return apart, copy

    sends = []
    for p in range(planes):
        moved = moved_plane(loads, p, coils, width_y, image_ref, sens_ref, kspace_ref, table_ref, step_ref[0], patterns)
        if p == 0:
            loads["shifts"].wait()
        for k in range(2):
            part = pltpu.roll(moved[k], shifts_ref[1], 1)
            wrapped[p, k, pl.ds(0, rows), :] = part[width_y - rows :]
            wrapped[p, k, pl.ds(rows, width_y), :] = part
            rolled[p, k] = wrapped[p, k, pl.ds(rows - shifts_ref[0], width_y), :]
        if p == 0:
            pl.semaphore_wait(barrier, total - 1)
        pltpu.make_async_copy(
            rolled.at[p, :, pl.ds(pl.multiple_of(me * rows, rows), rows), :],
            gathered.at[p, part_me, frame_me],
            recv_out.at[p, frame_me, part_me],
        ).start()
        for f, q, maybe in order_out(p):
            sends.append(send(p, f, q, maybe))

    pairs = [(f, g) for f in range(frames) for g in range(f + 1)]
    for p in range(planes):
        for f, q in everyone:
            place = gathered.at[p, q, f]
            pltpu.make_async_copy(place, place, recv_out.at[p, f, q]).wait()
        for n, (f, g) in enumerate(pairs):
            sum_re = None
            sum_im = None
            for q in range(group):
                f_re, f_im = gathered[p, q, f, 0], gathered[p, q, f, 1]
                g_re, g_im = gathered[p, q, g, 0], gathered[p, q, g, 1]
                re = f_re * g_re + f_im * g_im
                sum_re = re if sum_re is None else sum_re + re
                if f != g:
                    im = f_im * g_re - f_re * g_im
                    sum_im = im if sum_im is None else sum_im + im
            spot = f * frames + g
            entries[spot] = sum_re if p == 0 else entries[spot] + sum_re
            if f != g:
                spot = g * frames + f
                entries[spot] = sum_im if p == 0 else entries[spot] + sum_im

    one_row = lax.broadcasted_iota(jnp.int32, (width_z, width_z), 0) // PATCH_Z
    one_lane = lax.broadcasted_iota(jnp.int32, (width_z, width_z), 1) // PATCH_Z
    same = (one_row == one_lane).astype(jnp.bfloat16)
    cells = entries[...]
    shift = rows // 2
    while shift:
        cells = cells + pltpu.roll(cells, shift, 1)
        shift //= 2
    high, low = halves(cells.reshape(frames * frames * rows, width_z))
    entries[...] = (mul(high, same) + mul(low, same)).reshape(frames * frames, rows, width_z)

    level = level_ref[0]
    matrix = {}
    for f, g in pairs:
        if f == g:
            matrix[f, f] = (entries[f * frames + f] + level, None)
        else:
            matrix[f, g] = (entries[f * frames + g], entries[g * frames + f])
    matrix = sweep(matrix, frames)
    for f, g in pairs:
        re, im = matrix[f, g]
        inverse[f, g, 0] = re * level
        if f != g:
            inverse[f, g, 1] = im * level
            inverse[g, f, 0] = re * level
            inverse[g, f, 1] = -im * level
        else:
            inverse[f, f, 1] = jnp.zeros_like(re)

    backs = []
    spot = pl.ds(pl.multiple_of(me * rows, rows), rows)
    for f in range(frames):
        weights = [(inverse[f, g, 0], inverse[f, g, 1]) for g in range(frames)]
        for q in range(group):
            for p in range(planes):
                re = gathered[p, q, f, 0]
                im = gathered[p, q, f, 1]
                for g in range(frames):
                    g_re, g_im = gathered[p, q, g, 0], gathered[p, q, g, 1]
                    w_re, w_im = weights[g]
                    re = re + (w_re * g_re - w_im * g_im)
                    im = im + (w_re * g_im + w_im * g_re)
                finished[q, f, p, 0] = re
                finished[q, f, p, 1] = im
            place = landed.at[:, :, spot, :]
            apart = other(f, q)
            copy = pltpu.make_async_remote_copy(
                src_ref=finished.at[q, f],
                dst_ref=place,
                send_sem=send_back.at[f, q],
                recv_sem=recv_back.at[frame_me, part_me],
                device_id={"plane": base + q, "frame": f},
                device_id_type=pl.DeviceIdType.MESH,
            )
            pl.when(apart)(copy.start)
            pl.when(jnp.logical_not(apart))(pltpu.make_async_copy(finished.at[q, f], place, recv_back.at[f, q]).start)
            backs.append((apart, copy))
    for apart, copy in sends:
        if apart is None:
            copy.wait_send()
        else:
            pl.when(apart)(copy.wait_send)
    for f, q in everyone:
        place = landed.at[:, :, pl.ds((f * group + q) * rows, rows), :]
        pltpu.make_async_copy(place, place, recv_back.at[f, q]).wait()
    shift_z = lax.rem(width_z - shifts_ref[1], width_z)
    for p in range(planes):
        for k in range(2):
            part = pltpu.roll(landed[p, k], shift_z, 1)
            wrapped[p, k, pl.ds(0, width_y), :] = part
            wrapped[p, k, pl.ds(width_y, rows), :] = part[:rows]
            out_ref[p, 0, k] = wrapped[p, k, pl.ds(shifts_ref[0], width_y), :]
    for apart, copy in backs:
        pl.when(apart)(copy.wait_send)


def local_fused(image, sens, kspace, offsets, shifts, step_size, threshold):
    planes, _, _, width_y, width_z = image.shape
    coils = sens.shape[0]
    frames = lax.axis_size("frame")
    group = PATCH_X // planes
    total = frames * group
    table = jnp.asarray(block_tables(width_y))
    vmem = pl.BlockSpec(memory_space=pltpu.VMEM)
    smem = pl.BlockSpec(memory_space=pltpu.SMEM)
    hbm = pl.BlockSpec(memory_space=pltpu.HBM)
    slab = (PATCH_Y, width_z)
    dma = pltpu.SemaphoreType.DMA
    in_hbm = [
        pltpu.with_memory_space_constraint(x, pltpu.HBM) for x in (shifts, offsets, image, sens, kspace, table)
    ]
    return pl.pallas_call(
        functools.partial(step_kernel, planes, frames, group, coils, width_y, width_z),
        out_shape=jax.ShapeDtypeStruct(image.shape, jnp.float32),
        in_specs=[smem, smem] + [hbm] * 6,
        out_specs=vmem,
        scratch_shapes=[
            pltpu.SMEM(shifts.shape, shifts.dtype),
            pltpu.VMEM(offsets.shape, offsets.dtype),
            pltpu.VMEM(image.shape, image.dtype),
            pltpu.VMEM(sens.shape, sens.dtype),
            pltpu.VMEM(kspace.shape, kspace.dtype),
            pltpu.VMEM(table.shape, table.dtype),
            pltpu.VMEM((4, 2 * width_y, 2 * width_y), table.dtype),
            dma((3 * planes + 3,)),
            pltpu.VMEM((planes, 2, width_y + PATCH_Y, width_z), jnp.float32),
            pltpu.VMEM((planes, 2, width_y, width_z), jnp.float32),
            pltpu.VMEM((planes, group, frames, 2) + slab, jnp.float32),
            pltpu.VMEM((frames * frames,) + slab, jnp.float32),
            pltpu.VMEM((frames, frames, 2) + slab, jnp.float32),
            pltpu.VMEM((group, frames, planes, 2) + slab, jnp.float32),
            pltpu.VMEM((planes, 2, width_y, width_z), jnp.float32),
            dma((planes, frames, group)),
            dma((planes, frames, group)),
            dma((frames, group)),
            dma((frames, group)),
        ],
        compiler_params=pltpu.CompilerParams(collective_id=0, has_side_effects=True, vmem_limit_bytes=VMEM_BYTES),
        name="prox_step",
    )(step_size, threshold, *in_hbm)


def local(image, sens, kspace, offsets, shifts, step_size, threshold):
    planes, frames_dev, _, width_y, width_z = image.shape
    frames = frames_dev * lax.axis_size("frame")
    group = PATCH_X // planes
    one_block = frames * group * PATCH_Y == width_y and frames_dev == 1 and frames & (frames - 1) == 0
    split = group > 1 and group & (group - 1) == 0 and lax.axis_size("plane") % group == 0
    if one_block and split and width_y == width_z and width_z % 128 == 0:
        return local_fused(image, sens, kspace, offsets, shifts, step_size, threshold)
    return local_general(image, sens, kspace, offsets, shifts, step_size, threshold)


def solution(mesh):
    in_specs = (
        P("plane", "frame", None, None, None),
        P(None, "plane", None, None, None),
        P(None, "plane", "frame", None, None, None),
        P("frame", None),
        P(),
        P(),
        P(),
    )
    out_specs = P("plane", "frame", None, None, None)
    return jax.shard_map(local, mesh=mesh, in_specs=in_specs, out_specs=out_specs, check_vma=False)
```

```python
import functools
import math

import jax
import jax.numpy as jnp
import numpy as np
from jax import lax
from jax.experimental import pallas as pl
from jax.experimental.pallas import tpu as pltpu
from jax.sharding import PartitionSpec as P

PATCH_X = 4
PATCH_Y = 8
PATCH_Z = 8
ACCEL = 4
CENTER = 8


def from_partner(block, axis, distance):
    count = lax.axis_size(axis)
    route = []
    for low in range(count):
        high = low | 1 << distance
        if high != low and high < count:
            route += [(low, high), (high, low)]
    return lax.ppermute(block, axis, route)


def dft_tables(length):
    indices = jnp.arange(length, dtype=jnp.int32)
    phases = indices[:, None] * indices[None, :] % length
    angles = phases.astype(jnp.float32) * (2.0 * math.pi / length)
    norm_scale = 1.0 / math.sqrt(length)
    return (jnp.cos(angles) * norm_scale, jnp.sin(angles) * norm_scale)


def along_z(stacked, right_table, sign, width_z):
    product = jnp.einsum(
        "...z,zw->...w",
        stacked,
        right_table,
        precision=lax.Precision.HIGHEST,
        preferred_element_type=jnp.float32,
    )
    cos_part = product[..., :width_z]
    sin_part = product[..., width_z:]
    real_part = cos_part[..., 0, :, :] + sign * sin_part[..., 1, :, :]
    imag_part = cos_part[..., 1, :, :] - sign * sin_part[..., 0, :, :]
    return jnp.stack([real_part, imag_part], axis=-3)


def along_y(stacked, left_table):
    shape_in = stacked.shape
    merged = stacked.reshape(shape_in[:-3] + (2 * shape_in[-2], shape_in[-1]))
    result = jnp.einsum(
        "ur,...rz->...uz",
        left_table,
        merged,
        precision=lax.Precision.HIGHEST,
        preferred_element_type=jnp.float32,
    )
    return result.reshape(shape_in)


def rotate(casorati):
    frames2, voxels = (casorati.shape[-2], casorati.shape[-1])
    split_parts = casorati.reshape(casorati.shape[:-2] + (frames2 // 2, 2, voxels))
    turned = jnp.stack([-split_parts[..., 1, :], split_parts[..., 0, :]], axis=-2)
    return turned.reshape(casorati.shape)


def gram_of(casorati):
    twin = rotate(casorati)
    first = jnp.einsum(
        "kav,kbv->kab",
        casorati,
        casorati,
        precision=lax.Precision.HIGHEST,
        preferred_element_type=jnp.float32,
    )
    second = jnp.einsum(
        "kav,kbv->kab",
        twin,
        twin,
        precision=lax.Precision.HIGHEST,
        preferred_element_type=jnp.float32,
    )
    return first + second


def shrink(casorati, gram, level):
    order = gram.shape[-1]
    system = gram + level * jnp.eye(order, dtype=jnp.float32)
    factor = jnp.linalg.cholesky(system)
    forward_part = jax.scipy.linalg.solve_triangular(factor, casorati, lower=True)
    solved = jax.scipy.linalg.solve_triangular(factor, forward_part, lower=True, trans=1)
    return casorati - level * solved


def local_general(image, sens, kspace, offsets, shifts, step_size, threshold):
    planes, frames_dev, _, width_y, width_z = image.shape
    frames = frames_dev * lax.axis_size("frame")
    cos_y, sin_y = dft_tables(width_y)
    cos_z, sin_z = dft_tables(width_z)
    right_table = jnp.concatenate([cos_z, sin_z], axis=1)
    left_forward = jnp.concatenate(
        [jnp.concatenate([cos_y, sin_y], axis=1), jnp.concatenate([-sin_y, cos_y], axis=1)], axis=0
    )
    left_inverse = jnp.concatenate(
        [jnp.concatenate([cos_y, -sin_y], axis=1), jnp.concatenate([sin_y, cos_y], axis=1)], axis=0
    )
    rows_y = jnp.arange(width_y, dtype=jnp.int32)
    rows_z = jnp.arange(width_z, dtype=jnp.int32)
    low_y = (rows_y < CENTER) | (rows_y >= width_y - CENTER)
    low_z = (rows_z < CENTER) | (rows_z >= width_z - CENTER)
    regular = (rows_z[None, None, :] + offsets[:, :, None]) % ACCEL == 0
    sampled = (regular | low_y[None, :, None] & low_z[None, None, :]).astype(jnp.float32)
    image_re = image[:, :, 0]
    image_im = image[:, :, 1]
    maps = sens.astype(jnp.float32)
    sens_re = maps[:, :, 0][:, :, None]
    sens_im = maps[:, :, 1][:, :, None]
    coil_re = sens_re * image_re[None] - sens_im * image_im[None]
    coil_im = sens_re * image_im[None] + sens_im * image_re[None]
    stacked = jnp.stack([coil_re, coil_im], axis=3)
    spectra = along_y(along_z(stacked, right_table, 1.0, width_z), left_forward)
    resid = sampled[None, None, :, None] * (spectra - kspace.astype(jnp.float32))
    returned = along_z(along_y(resid, left_inverse), right_table, -1.0, width_z)
    back_re = returned[:, :, :, 0]
    back_im = returned[:, :, :, 1]
    grad_re = jnp.sum(sens_re * back_re + sens_im * back_im, axis=0)
    grad_im = jnp.sum(sens_re * back_im - sens_im * back_re, axis=0)
    moved = image - step_size[0] * jnp.stack([grad_re, grad_im], axis=2)
    rolled = jnp.roll(moved, (shifts[0], shifts[1]), axis=(3, 4))
    nyb = width_y // PATCH_Y
    nzb = width_z // PATCH_Z
    voxels = planes * PATCH_Y * PATCH_Z
    blocks = rolled.reshape(planes, frames_dev, 2, nyb, PATCH_Y, nzb, PATCH_Z)
    blocks = blocks.transpose(3, 5, 1, 2, 0, 4, 6).reshape(nyb * nzb, frames_dev, 2, voxels)
    regrouped = lax.all_to_all(blocks, "frame", split_axis=0, concat_axis=1, tiled=True)
    count = regrouped.shape[0]
    casorati = regrouped.reshape(count, 2 * frames, voxels)
    level = threshold[0]
    parity = lax.axis_index("plane") % 2
    halfway = count // 2
    first_part = casorati[:halfway]
    second_part = casorati[halfway:]
    kept_part = jnp.where(parity == 0, first_part, second_part)
    outgoing = jnp.where(parity == 0, second_part, first_part)
    incoming = from_partner(outgoing, "plane", 0)
    complete = jnp.concatenate([kept_part, incoming], axis=2)
    finished = shrink(complete, gram_of(complete), level)
    own_part = finished[:, :, :voxels]
    returned_part = from_partner(finished[:, :, voxels:], "plane", 0)
    shrunk = jnp.where(
        parity == 0,
        jnp.concatenate([own_part, returned_part], axis=0),
        jnp.concatenate([returned_part, own_part], axis=0),
    )
    restored = lax.all_to_all(
        shrunk.reshape(count, frames, 2, voxels), "frame", split_axis=1, concat_axis=0, tiled=True
    )
    placed = restored.reshape(nyb, nzb, frames_dev, 2, planes, PATCH_Y, PATCH_Z)
    placed = placed.transpose(4, 2, 3, 0, 5, 1, 6).reshape(planes, frames_dev, 2, width_y, width_z)
    return jnp.roll(placed, (-shifts[0], -shifts[1]), axis=(3, 4))


VMEM_BYTES = 24 * 1024 * 1024


PLAN = [[(0, 'a'), (0, 'c'), (0, 'b'), (0, 'd')], [(1, 'a'), (1, 'c'), (1, 'b'), (1, 'd')]]


def two_parts(table):
    high = table.astype(jnp.bfloat16)
    return high, (table - high.astype(np.float64)).astype(jnp.bfloat16)


def block_tables(length):
    indices = np.arange(length)
    angles = (indices[:, None] * indices[None, :] % length) * (2.0 * np.pi / length)
    cos = np.cos(angles) / np.sqrt(length)
    sin = np.sin(angles) / np.sqrt(length)
    centre = np.concatenate([indices[:CENTER], indices[length - CENTER :]])
    into = np.block([[cos, -sin], [sin, cos]])[:, np.concatenate([centre, length + centre])]
    into_high, into_low = two_parts(into)
    from_high, from_low = two_parts(into.T)
    rest = length - 4 * len(centre)
    into = np.concatenate([into_high, into_low, np.zeros((2 * length, rest), jnp.bfloat16)], axis=1)
    rest = length - 6 * len(centre)
    back = np.concatenate([from_high, from_low, from_high, np.zeros((rest, 2 * length), jnp.bfloat16)], axis=0)
    whole = np.concatenate([*two_parts(cos), *two_parts(sin)], axis=0)
    return np.concatenate([whole, into, back[:, :length], back[:, length:]], axis=0)


def lay_tables(parts_ref, table_ref, width):
    low, top = pl.ds(0, width), pl.ds(width, width)
    for k in range(2):
        cos, sin = parts_ref[pl.ds(k * width, width)], parts_ref[pl.ds((2 + k) * width, width)]
        for table, upper, lower in ((0, sin, -sin), (1, -sin, sin)):
            first, second = pl.ds(2 * k * width, width), pl.ds((2 * k + 1) * width, width)
            table_ref[table, first, low] = cos
            table_ref[table, second, top] = cos
            table_ref[table, first, top] = upper
            table_ref[table, second, low] = lower


def halves(values):
    high = values.astype(jnp.bfloat16)
    return high, (values - high.astype(jnp.float32)).astype(jnp.bfloat16)


def mul(left, right):
    return jnp.dot(left, right, preferred_element_type=jnp.float32)


def from_left(table, values):
    count = table.shape[1]
    value_high, value_low = halves(values)
    first = mul(table, value_high)
    return first[:count] + (first[count:] + mul(table[:count], value_low))


def row_patterns(offsets_ref, offset_rows, width_y, width_z):
    lane = lax.broadcasted_iota(jnp.int32, (width_y, width_z), 1)
    row = lax.broadcasted_iota(jnp.int32, (width_y, width_z), 0)
    offset = jnp.broadcast_to(offsets_ref[...].astype(jnp.float32), (width_z, width_y)).T
    wanted = jnp.where(offset == 0.0, 0.0, ACCEL - offset)
    regular = lax.rem(lane, ACCEL).astype(jnp.float32) == wanted
    low_y = (row < CENTER) | (row >= width_y - CENTER)
    low_z = (lane < CENTER) | (lane >= width_z - CENTER)
    centre = low_y & low_z
    scale = float(ACCEL)
    kept = jnp.where(regular | centre, scale, 0.0).astype(jnp.bfloat16)
    extra = jnp.where(centre & jnp.logical_not(regular), scale, 0.0)
    edge = jnp.concatenate([extra[:CENTER], extra[width_y - CENTER :]], axis=0)
    edge = jnp.where(lane[: 2 * CENTER] < CENTER, edge, pltpu.roll(edge, 2 * CENTER, 1))
    slot = lane[: 2 * CENTER]
    edge = jnp.where(slot < 2 * CENTER, edge, jnp.where(slot < 4 * CENTER, pltpu.roll(edge, 2 * CENTER, 1), 0.0))
    half = jnp.where((offset == 0.0) | (offset == 2.0), 1.0, -1.0)
    real = jnp.where(offset == 0.0, 1.0, jnp.where(offset == 2.0, -1.0, 0.0))
    imag = jnp.where(offset == 1.0, -1.0, jnp.where(offset == 3.0, 1.0, 0.0))
    return kept, edge, half, real, imag


def moved_plane(loads, start_later, p, coils, width, image_ref, sens_ref, kspace_ref, parts_ref, table_ref, step, patterns):
    kept, edge, half, real, imag = patterns
    loads["kspace", p].wait()
    data = jnp.concatenate(
        [
            jnp.concatenate([kspace_ref[c, p, 0, k] * kept for k in range(2)], axis=1)
            for c in range(coils)
        ],
        axis=0,
    )
    known = mul(data, table_ref[0, : 2 * width]) + mul(data, table_ref[0, 2 * width :])
    loads["image", p].wait()
    loads["sens", p].wait()
    if p == 0:
        start_later()
    image_re = image_ref[p, 0, 0]
    image_im = image_ref[p, 0, 1]
    coil_re, coil_im = [], []
    for c in range(coils):
        sens_re = sens_ref[c, p, 0].astype(jnp.float32)
        sens_im = sens_ref[c, p, 1].astype(jnp.float32)
        coil_re.append(sens_re * image_re - sens_im * image_im)
        coil_im.append(sens_re * image_im + sens_im * image_re)
    stacked = jnp.concatenate([jnp.concatenate(coil_re, axis=1), jnp.concatenate(coil_im, axis=1)], axis=0)
    lines = from_left(table_ref[0], stacked)

    def part(k, c):
        return lines[k * width : (k + 1) * width, c * width : (c + 1) * width]

    low = jnp.concatenate(
        [
            jnp.concatenate(
                [jnp.concatenate([part(k, c)[:CENTER], part(k, c)[width - CENTER :]], axis=0) for k in range(2)], axis=1
            )
            for c in range(coils)
        ],
        axis=0,
    )
    weight = jnp.concatenate([edge] * coils, axis=0)
    into = parts_ref[pl.ds(4 * width, 2 * width)]
    out = jnp.concatenate([parts_ref[pl.ds(6 * width, width)], parts_ref[pl.ds(7 * width, width)]], axis=1)
    found = mul(jnp.concatenate(halves(low), axis=0), into)
    found = found[: low.shape[0]] + found[low.shape[0] :]
    found = weight * (found + pltpu.roll(found, width - 4 * CENTER, 1))
    found_high = found.astype(jnp.bfloat16).astype(jnp.float32)
    three = found_high + pltpu.roll(found_high, 4 * CENTER, 1) + pltpu.roll(found - found_high, 8 * CENTER, 1)
    added = mul(three.astype(jnp.bfloat16), out)
    resid_re, resid_im = [], []
    for c in range(coils):
        both = []
        for k in range(2):
            line = part(k, c)
            both.append(line + half * pltpu.roll(line, width // 2, 1))
        turned = [pltpu.roll(line, width // 4, 1) for line in both]
        sums = [
            both[0] + (real * turned[0] - imag * turned[1]),
            both[1] + (real * turned[1] + imag * turned[0]),
        ]
        for k, out in ((0, resid_re), (1, resid_im)):
            value = sums[k] - known[c * width : (c + 1) * width, k * width : (k + 1) * width]
            more = added[2 * CENTER * c : 2 * CENTER * (c + 1), k * width : (k + 1) * width]
            out.append(
                jnp.concatenate(
                    [
                        value[:CENTER] + more[:CENTER],
                        value[CENTER : width - CENTER],
                        value[width - CENTER :] + more[CENTER:],
                    ],
                    axis=0,
                )
            )
    resid = jnp.concatenate([jnp.concatenate(resid_re, axis=1), jnp.concatenate(resid_im, axis=1)], axis=0)
    back = from_left(table_ref[1], resid)
    grad_re = jnp.zeros_like(image_re)
    grad_im = jnp.zeros_like(image_im)
    for c in range(coils):
        back_re = back[:width, c * width : (c + 1) * width]
        back_im = back[width:, c * width : (c + 1) * width]
        sens_re = sens_ref[c, p, 0].astype(jnp.float32)
        sens_im = sens_ref[c, p, 1].astype(jnp.float32)
        grad_re += sens_re * back_re + sens_im * back_im
        grad_im += sens_re * back_im - sens_im * back_re
    scaled = step * (1.0 / ACCEL)
    return image_re - scaled * grad_re, image_im - scaled * grad_im


def sweep(matrix, order):
    for k in range(order):
        pivot = 1.0 / matrix[k, k][0]
        column = {}
        for i in range(order):
            if i > k:
                column[i] = matrix[i, k]
            elif i < k:
                column[i] = (matrix[k, i][0], -matrix[k, i][1])
        scaled = {i: (re * pivot, im * pivot) for i, (re, im) in column.items()}
        for i in column:
            for j in column:
                if j > i:
                    continue
                a_re, a_im = scaled[i]
                b_re, b_im = column[j]
                re, im = matrix[i, j]
                re = re - (a_re * b_re + a_im * b_im)
                if i != j:
                    im = im - (a_im * b_re - a_re * b_im)
                matrix[i, j] = (re, im)
        for i in column:
            if i > k:
                matrix[i, k] = scaled[i]
            else:
                matrix[k, i] = (scaled[i][0], -scaled[i][1])
        matrix[k, k] = (-pivot, None)
    return matrix


def step_kernel(
    planes, frames, group, coils, width_y, width_z,
    step_ref, level_ref, shifts_hbm, offsets_hbm, image_hbm, sens_hbm, kspace_hbm, table_hbm,
    out_ref,
    shifts_ref, offsets_ref, image_ref, sens_ref, kspace_ref, parts_ref, table_ref, load_sem,
    wrapped, rolled, gathered, entries, inverse, finished, landed,
    send_out, recv_out, send_back, recv_back,
):
    total = frames * group
    plane_me = lax.axis_index("plane")
    frame_me = lax.axis_index("frame")
    part_me = lax.rem(plane_me, group)
    base = plane_me - part_me
    me = frame_me * group + part_me
    rows = PATCH_Y
    everyone = [(f, q) for f in range(frames) for q in range(group)]

    def other(f, q):
        return (frame_me != f) | (part_me != q)

    barrier = pltpu.get_barrier_semaphore()
    for f, q in everyone:

        @pl.when(other(f, q))
        def _():
            pl.semaphore_signal(
                barrier, inc=1, device_id={"plane": base + q, "frame": f}, device_id_type=pl.DeviceIdType.MESH
            )

    loads = {}

    def load(name, source, target):
        loads[name] = pltpu.make_async_copy(source, target, load_sem.at[len(loads)])
        loads[name].start()

    load("offsets", offsets_hbm, offsets_ref)
    load("table", table_hbm, parts_ref)

    def load_plane(p):
        load(("kspace", p), kspace_hbm.at[:, p], kspace_ref.at[:, p])
        load(("image", p), image_hbm.at[p], image_ref.at[p])
        load(("sens", p), sens_hbm.at[:, p], sens_ref.at[:, p])

    load_plane(0)
    load("shifts", shifts_hbm, shifts_ref)

    def start_later():
        for p in range(1, planes):
            load_plane(p)

    loads["offsets"].wait()
    patterns = row_patterns(offsets_ref, None, width_y, width_z)
    loads["table"].wait()
    lay_tables(parts_ref, table_ref, width_y)

    half, quarter = frames // 2, frames // 4
    far = frame_me // half
    near = 1 - far
    step_in = lax.rem(frame_me // quarter, 2)
    inner = lax.rem(frame_me, quarter)

    def order_out(token):
        zone, only = token[0], token[1:]
        z_high, z_low, maybe = {
            "a": (near, far, False), "b": (near, near, False), "c": (far, near, True), "d": (far, far, True),
            "3": (near, 1 - step_in, False), "2": (near, step_in, False), "1": (far, 1 - step_in, False), "0": (far, step_in, True),
        }[zone]
        for k in reversed(range(quarter)):
            x = lax.rem(inner + k, quarter)
            if only in ("0", "1"):
                yield z_high * half + z_low * quarter + x, int(only), maybe and k == 0
                continue
            for r in reversed(range(group)):
                q = lax.rem(part_me + r, group)
                yield z_high * half + z_low * quarter + x, q, maybe and k == 0 and r == 0

    def send(p, f, q, maybe):
        block = rolled.at[p, :, pl.ds(pl.multiple_of((f * group + q) * rows, rows), rows), :]
        copy = pltpu.make_async_remote_copy(
            src_ref=block,
            dst_ref=gathered.at[p, part_me, frame_me],
            send_sem=send_out.at[p],
            recv_sem=recv_out.at[p],
            device_id={"plane": base + q, "frame": f},
            device_id_type=pl.DeviceIdType.MESH,
        )
        if maybe:
            pl.when(other(f, q))(copy.start)
        else:
            copy.start()

    def landed_all(ref, sem):
        pltpu.make_async_copy(ref, ref, sem).wait()

    for p in range(planes):
        moved = moved_plane(loads, start_later, p, coils, width_y, image_ref, sens_ref, kspace_ref, parts_ref, table_ref, step_ref[0], patterns)
        if p == 0:
            loads["shifts"].wait()
        for k in range(2):
            part = pltpu.roll(moved[k], shifts_ref[1], 1)
            wrapped[p, k, pl.ds(0, rows), :] = part[width_y - rows :]
            wrapped[p, k, pl.ds(rows, width_y), :] = part
            rolled[p, k] = wrapped[p, k, pl.ds(rows - shifts_ref[0], width_y), :]
        if p == 0:
            pl.semaphore_wait(barrier, total - 1)
        pltpu.make_async_copy(
            rolled.at[p, :, pl.ds(pl.multiple_of(me * rows, rows), rows), :],
            gathered.at[p, part_me, frame_me],
            recv_out.at[p],
        ).start()
        for wp, zone in PLAN[p]:
            for f, q, maybe in order_out(zone):
                send(wp, f, q, maybe)

    pairs = [(f, g) for f in range(frames) for g in range(f + 1)]
    for p in range(planes):
        landed_all(gathered.at[p], recv_out.at[p])
        for n, (f, g) in enumerate(pairs):
            sum_re = None
            sum_im = None
            for q in range(group):
                f_re, f_im = gathered[p, q, f, 0], gathered[p, q, f, 1]
                g_re, g_im = gathered[p, q, g, 0], gathered[p, q, g, 1]
                re = f_re * g_re + f_im * g_im
                sum_re = re if sum_re is None else sum_re + re
                if f != g:
                    im = f_im * g_re - f_re * g_im
                    sum_im = im if sum_im is None else sum_im + im
            spot = f * frames + g
            entries[spot] = sum_re if p == 0 else entries[spot] + sum_re
            if f != g:
                spot = g * frames + f
                entries[spot] = sum_im if p == 0 else entries[spot] + sum_im

    one_row = lax.broadcasted_iota(jnp.int32, (width_z, width_z), 0) // PATCH_Z
    one_lane = lax.broadcasted_iota(jnp.int32, (width_z, width_z), 1) // PATCH_Z
    same = (one_row == one_lane).astype(jnp.bfloat16)
    cells = entries[...]
    shift = rows // 2
    while shift:
        cells = cells + pltpu.roll(cells, shift, 1)
        shift //= 2
    high, low = halves(cells.reshape(frames * frames * rows, width_z))
    entries[...] = (mul(high, same) + mul(low, same)).reshape(frames * frames, rows, width_z)

    level = level_ref[0]
    matrix = {}
    for f, g in pairs:
        if f == g:
            matrix[f, f] = (entries[f * frames + f] + level, None)
        else:
            matrix[f, g] = (entries[f * frames + g], entries[g * frames + f])
    matrix = sweep(matrix, frames)
    for f, g in pairs:
        re, im = matrix[f, g]
        inverse[f, g, 0] = re * level
        if f != g:
            inverse[f, g, 1] = im * level
            inverse[g, f, 0] = re * level
            inverse[g, f, 1] = -im * level
        else:
            inverse[f, f, 1] = jnp.zeros_like(re)

    spot = pl.ds(pl.multiple_of(me * rows, rows), rows)
    for f in range(frames):
        weights = [(inverse[f, g, 0], inverse[f, g, 1]) for g in range(frames)]
        for q in range(group):
            for p in range(planes):
                re = gathered[p, q, f, 0]
                im = gathered[p, q, f, 1]
                for g in range(frames):
                    g_re, g_im = gathered[p, q, g, 0], gathered[p, q, g, 1]
                    w_re, w_im = weights[g]
                    re = re + (w_re * g_re - w_im * g_im)
                    im = im + (w_re * g_im + w_im * g_re)
                finished[q, f, p, 0] = re
                finished[q, f, p, 1] = im
            place = landed.at[:, :, spot, :]
            apart = other(f, q)
            copy = pltpu.make_async_remote_copy(
                src_ref=finished.at[q, f],
                dst_ref=place,
                send_sem=send_back,
                recv_sem=recv_back,
                device_id={"plane": base + q, "frame": f},
                device_id_type=pl.DeviceIdType.MESH,
            )
            pl.when(apart)(copy.start)
            pl.when(jnp.logical_not(apart))(pltpu.make_async_copy(finished.at[q, f], place, recv_back).start)
    sent = pl.ds(0, (total - 1) * rows)
    for p in range(planes):
        landed_all(rolled.at[p, :, sent, :], send_out.at[p])
    landed_all(landed, recv_back)
    shift_z = lax.rem(width_z - shifts_ref[1], width_z)
    for p in range(planes):
        for k in range(2):
            part = pltpu.roll(landed[p, k], shift_z, 1)
            wrapped[p, k, pl.ds(0, width_y), :] = part
            wrapped[p, k, pl.ds(width_y, rows), :] = part[:rows]
            out_ref[p, 0, k] = wrapped[p, k, pl.ds(shifts_ref[0], width_y), :]
    landed_all(landed.at[:, :, sent, :], send_back)


def local_fused(image, sens, kspace, offsets, shifts, step_size, threshold):
    planes, _, _, width_y, width_z = image.shape
    coils = sens.shape[0]
    frames = lax.axis_size("frame")
    group = PATCH_X // planes
    total = frames * group
    table = jnp.asarray(block_tables(width_y))
    vmem = pl.BlockSpec(memory_space=pltpu.VMEM)
    smem = pl.BlockSpec(memory_space=pltpu.SMEM)
    hbm = pl.BlockSpec(memory_space=pltpu.HBM)
    slab = (PATCH_Y, width_z)
    dma = pltpu.SemaphoreType.DMA
    in_hbm = [
        pltpu.with_memory_space_constraint(x, pltpu.HBM) for x in (shifts, offsets, image, sens, kspace, table)
    ]
    return pl.pallas_call(
        functools.partial(step_kernel, planes, frames, group, coils, width_y, width_z),
        out_shape=jax.ShapeDtypeStruct(image.shape, jnp.float32),
        in_specs=[smem, smem] + [hbm] * 6,
        out_specs=vmem,
        scratch_shapes=[
            pltpu.SMEM(shifts.shape, shifts.dtype),
            pltpu.VMEM(offsets.shape, offsets.dtype),
            pltpu.VMEM(image.shape, image.dtype),
            pltpu.VMEM(sens.shape, sens.dtype),
            pltpu.VMEM(kspace.shape, kspace.dtype),
            pltpu.VMEM(table.shape, table.dtype),
            pltpu.VMEM((2, 4 * width_y, 2 * width_y), table.dtype),
            dma((3 * planes + 3,)),
            pltpu.VMEM((planes, 2, width_y + PATCH_Y, width_z), jnp.float32),
            pltpu.VMEM((planes, 2, width_y, width_z), jnp.float32),
            pltpu.VMEM((planes, group, frames, 2) + slab, jnp.float32),
            pltpu.VMEM((frames * frames,) + slab, jnp.float32),
            pltpu.VMEM((frames, frames, 2) + slab, jnp.float32),
            pltpu.VMEM((group, frames, planes, 2) + slab, jnp.float32),
            pltpu.VMEM((planes, 2, width_y, width_z), jnp.float32),
            dma((planes,)),
            dma((planes,)),
            dma(()),
            dma(()),
        ],
        compiler_params=pltpu.CompilerParams(collective_id=0, has_side_effects=True, vmem_limit_bytes=VMEM_BYTES),
        name="prox_step",
    )(step_size, threshold, *in_hbm)


def local(image, sens, kspace, offsets, shifts, step_size, threshold):
    planes, frames_dev, _, width_y, width_z = image.shape
    frames = frames_dev * lax.axis_size("frame")
    group = PATCH_X // planes
    one_block = frames * group * PATCH_Y == width_y and frames_dev == 1 and frames & (frames - 1) == 0
    split = group > 1 and group & (group - 1) == 0 and lax.axis_size("plane") % group == 0
    if one_block and split and width_y == width_z and width_z % 128 == 0:
        return local_fused(image, sens, kspace, offsets, shifts, step_size, threshold)
    return local_general(image, sens, kspace, offsets, shifts, step_size, threshold)


def solution(mesh):
    in_specs = (
        P("plane", "frame", None, None, None),
        P(None, "plane", None, None, None),
        P(None, "plane", "frame", None, None, None),
        P("frame", None),
        P(),
        P(),
        P(),
    )
    out_specs = P("plane", "frame", None, None, None)
    return jax.shard_map(local, mesh=mesh, in_specs=in_specs, out_specs=out_specs, check_vma=False)
```

```python
import functools
import math

import jax
import jax.numpy as jnp
import numpy as np
from jax import lax
from jax.experimental import pallas as pl
from jax.experimental.pallas import tpu as pltpu
from jax.sharding import PartitionSpec as P

PATCH_X = 4
PATCH_Y = 8
PATCH_Z = 8
ACCEL = 4
CENTER = 8
PAIR = 2


def from_partner(block, axis, distance):
    count = lax.axis_size(axis)
    route = []
    for low in range(count):
        high = low | 1 << distance
        if high != low and high < count:
            route += [(low, high), (high, low)]
    return lax.ppermute(block, axis, route)


def dft_tables(length):
    indices = jnp.arange(length, dtype=jnp.int32)
    phases = indices[:, None] * indices[None, :] % length
    angles = phases.astype(jnp.float32) * (2.0 * math.pi / length)
    norm_scale = 1.0 / math.sqrt(length)
    return (jnp.cos(angles) * norm_scale, jnp.sin(angles) * norm_scale)


def along_z(stacked, right_table, sign, width_z):
    product = jnp.einsum(
        "...z,zw->...w",
        stacked,
        right_table,
        precision=lax.Precision.HIGHEST,
        preferred_element_type=jnp.float32,
    )
    cos_part = product[..., :width_z]
    sin_part = product[..., width_z:]
    real_part = cos_part[..., 0, :, :] + sign * sin_part[..., 1, :, :]
    imag_part = cos_part[..., 1, :, :] - sign * sin_part[..., 0, :, :]
    return jnp.stack([real_part, imag_part], axis=-3)


def along_y(stacked, left_table):
    shape_in = stacked.shape
    merged = stacked.reshape(shape_in[:-3] + (2 * shape_in[-2], shape_in[-1]))
    result = jnp.einsum(
        "ur,...rz->...uz",
        left_table,
        merged,
        precision=lax.Precision.HIGHEST,
        preferred_element_type=jnp.float32,
    )
    return result.reshape(shape_in)


def rotate(casorati):
    frames2, voxels = (casorati.shape[-2], casorati.shape[-1])
    split_parts = casorati.reshape(casorati.shape[:-2] + (frames2 // 2, 2, voxels))
    turned = jnp.stack([-split_parts[..., 1, :], split_parts[..., 0, :]], axis=-2)
    return turned.reshape(casorati.shape)


def gram_of(casorati):
    twin = rotate(casorati)
    first = jnp.einsum(
        "kav,kbv->kab",
        casorati,
        casorati,
        precision=lax.Precision.HIGHEST,
        preferred_element_type=jnp.float32,
    )
    second = jnp.einsum(
        "kav,kbv->kab",
        twin,
        twin,
        precision=lax.Precision.HIGHEST,
        preferred_element_type=jnp.float32,
    )
    return first + second


def shrink(casorati, gram, level):
    order = gram.shape[-1]
    system = gram + level * jnp.eye(order, dtype=jnp.float32)
    factor = jnp.linalg.cholesky(system)
    forward_part = jax.scipy.linalg.solve_triangular(factor, casorati, lower=True)
    solved = jax.scipy.linalg.solve_triangular(factor, forward_part, lower=True, trans=1)
    return casorati - level * solved


def local_general(image, sens, kspace, offsets, shifts, step_size, threshold):
    planes, frames_dev, _, width_y, width_z = image.shape
    frames = frames_dev * lax.axis_size("frame")
    cos_y, sin_y = dft_tables(width_y)
    cos_z, sin_z = dft_tables(width_z)
    right_table = jnp.concatenate([cos_z, sin_z], axis=1)
    left_forward = jnp.concatenate(
        [jnp.concatenate([cos_y, sin_y], axis=1), jnp.concatenate([-sin_y, cos_y], axis=1)], axis=0
    )
    left_inverse = jnp.concatenate(
        [jnp.concatenate([cos_y, -sin_y], axis=1), jnp.concatenate([sin_y, cos_y], axis=1)], axis=0
    )
    rows_y = jnp.arange(width_y, dtype=jnp.int32)
    rows_z = jnp.arange(width_z, dtype=jnp.int32)
    low_y = (rows_y < CENTER) | (rows_y >= width_y - CENTER)
    low_z = (rows_z < CENTER) | (rows_z >= width_z - CENTER)
    regular = (rows_z[None, None, :] + offsets[:, :, None]) % ACCEL == 0
    sampled = (regular | low_y[None, :, None] & low_z[None, None, :]).astype(jnp.float32)
    image_re = image[:, :, 0]
    image_im = image[:, :, 1]
    maps = sens.astype(jnp.float32)
    sens_re = maps[:, :, 0][:, :, None]
    sens_im = maps[:, :, 1][:, :, None]
    coil_re = sens_re * image_re[None] - sens_im * image_im[None]
    coil_im = sens_re * image_im[None] + sens_im * image_re[None]
    stacked = jnp.stack([coil_re, coil_im], axis=3)
    spectra = along_y(along_z(stacked, right_table, 1.0, width_z), left_forward)
    resid = sampled[None, None, :, None] * (spectra - kspace.astype(jnp.float32))
    returned = along_z(along_y(resid, left_inverse), right_table, -1.0, width_z)
    back_re = returned[:, :, :, 0]
    back_im = returned[:, :, :, 1]
    grad_re = jnp.sum(sens_re * back_re + sens_im * back_im, axis=0)
    grad_im = jnp.sum(sens_re * back_im - sens_im * back_re, axis=0)
    moved = image - step_size[0] * jnp.stack([grad_re, grad_im], axis=2)
    rolled = jnp.roll(moved, (shifts[0], shifts[1]), axis=(3, 4))
    nyb = width_y // PATCH_Y
    nzb = width_z // PATCH_Z
    voxels = planes * PATCH_Y * PATCH_Z
    blocks = rolled.reshape(planes, frames_dev, 2, nyb, PATCH_Y, nzb, PATCH_Z)
    blocks = blocks.transpose(3, 5, 1, 2, 0, 4, 6).reshape(nyb * nzb, frames_dev, 2, voxels)
    regrouped = lax.all_to_all(blocks, "frame", split_axis=0, concat_axis=1, tiled=True)
    count = regrouped.shape[0]
    casorati = regrouped.reshape(count, 2 * frames, voxels)
    level = threshold[0]
    parity = lax.axis_index("plane") % 2
    halfway = count // 2
    first_part = casorati[:halfway]
    second_part = casorati[halfway:]
    kept_part = jnp.where(parity == 0, first_part, second_part)
    outgoing = jnp.where(parity == 0, second_part, first_part)
    incoming = from_partner(outgoing, "plane", 0)
    complete = jnp.concatenate([kept_part, incoming], axis=2)
    finished = shrink(complete, gram_of(complete), level)
    own_part = finished[:, :, :voxels]
    returned_part = from_partner(finished[:, :, voxels:], "plane", 0)
    shrunk = jnp.where(
        parity == 0,
        jnp.concatenate([own_part, returned_part], axis=0),
        jnp.concatenate([returned_part, own_part], axis=0),
    )
    restored = lax.all_to_all(
        shrunk.reshape(count, frames, 2, voxels), "frame", split_axis=1, concat_axis=0, tiled=True
    )
    placed = restored.reshape(nyb, nzb, frames_dev, 2, planes, PATCH_Y, PATCH_Z)
    placed = placed.transpose(4, 2, 3, 0, 5, 1, 6).reshape(planes, frames_dev, 2, width_y, width_z)
    return jnp.roll(placed, (-shifts[0], -shifts[1]), axis=(3, 4))


VMEM_BYTES = 24 * 1024 * 1024


PLAN = [[(0, 'W'), (0, 'Y'), (0, 'X'), (0, 'Z')], [(1, 'W'), (1, 'Y'), (1, 'X'), (1, 'Z')]]


def two_parts(table):
    high = table.astype(jnp.bfloat16)
    return high, (table - high.astype(np.float64)).astype(jnp.bfloat16)


def block_tables(length):
    indices = np.arange(length)
    angles = (indices[:, None] * indices[None, :] % length) * (2.0 * np.pi / length)
    cos = np.cos(angles) / np.sqrt(length)
    sin = np.sin(angles) / np.sqrt(length)
    centre = np.concatenate([indices[:CENTER], indices[length - CENTER :]])
    into = np.block([[cos, -sin], [sin, cos]])[:, np.concatenate([centre, length + centre])]
    into_high, into_low = two_parts(into)
    from_high, from_low = two_parts(into.T)
    rest = length - 4 * len(centre)
    into = np.concatenate([into_high, into_low, np.zeros((2 * length, rest), jnp.bfloat16)], axis=1)
    rest = length - 6 * len(centre)
    back = np.concatenate([from_high, from_low, from_high, np.zeros((rest, 2 * length), jnp.bfloat16)], axis=0)
    whole = np.concatenate([*two_parts(cos), *two_parts(sin)], axis=0)
    return np.concatenate([whole, into, back[:, :length], back[:, length:]], axis=0)


def lay_tables(parts_ref, table_ref, width):
    low, top = pl.ds(0, width), pl.ds(width, width)
    for k in range(2):
        cos, sin = parts_ref[pl.ds(k * width, width)], parts_ref[pl.ds((2 + k) * width, width)]
        for table, upper, lower in ((0, sin, -sin), (1, -sin, sin)):
            first, second = pl.ds(2 * k * width, width), pl.ds((2 * k + 1) * width, width)
            table_ref[table, first, low] = cos
            table_ref[table, second, top] = cos
            table_ref[table, first, top] = upper
            table_ref[table, second, low] = lower


def halves(values):
    high = values.astype(jnp.bfloat16)
    return high, (values - high.astype(jnp.float32)).astype(jnp.bfloat16)


def mul(left, right):
    return jnp.dot(left, right, preferred_element_type=jnp.float32)


def from_left(table, values):
    count = table.shape[1]
    value_high, value_low = halves(values)
    first = mul(table, value_high)
    return first[:count] + (first[count:] + mul(table[:count], value_low))


def row_patterns(offsets_ref, offset_rows, width_y, width_z):
    lane = lax.broadcasted_iota(jnp.int32, (width_y, width_z), 1)
    row = lax.broadcasted_iota(jnp.int32, (width_y, width_z), 0)
    offset = jnp.broadcast_to(offsets_ref[...].astype(jnp.float32), (width_z, width_y)).T
    wanted = jnp.where(offset == 0.0, 0.0, ACCEL - offset)
    regular = lax.rem(lane, ACCEL).astype(jnp.float32) == wanted
    low_y = (row < CENTER) | (row >= width_y - CENTER)
    low_z = (lane < CENTER) | (lane >= width_z - CENTER)
    centre = low_y & low_z
    scale = float(ACCEL)
    kept = jnp.where(regular | centre, scale, 0.0).astype(jnp.bfloat16)
    extra = jnp.where(centre & jnp.logical_not(regular), scale, 0.0)
    edge = jnp.concatenate([extra[:CENTER], extra[width_y - CENTER :]], axis=0)
    edge = jnp.where(lane[: 2 * CENTER] < CENTER, edge, pltpu.roll(edge, 2 * CENTER, 1))
    slot = lane[: 2 * CENTER]
    edge = jnp.where(slot < 2 * CENTER, edge, jnp.where(slot < 4 * CENTER, pltpu.roll(edge, 2 * CENTER, 1), 0.0))
    half = jnp.where((offset == 0.0) | (offset == 2.0), 1.0, -1.0)
    real = jnp.where(offset == 0.0, 1.0, jnp.where(offset == 2.0, -1.0, 0.0))
    imag = jnp.where(offset == 1.0, -1.0, jnp.where(offset == 3.0, 1.0, 0.0))
    return kept, edge, half, real, imag


def moved_plane(loads, start_later, p, coils, width, image_ref, sens_ref, kspace_ref, parts_ref, table_ref, step, patterns):
    kept, edge, half, real, imag = patterns
    sides = [range(c, min(c + PAIR, coils)) for c in range(0, coils, PAIR)]
    loads["kspace", p].wait()
    known = []
    for side in sides:
        data = jnp.concatenate(
            [jnp.concatenate([kspace_ref[c, p, 0, k] * kept for k in range(2)], axis=1) for c in side], axis=0
        )
        known.append(mul(data, table_ref[0, : 2 * width]) + mul(data, table_ref[0, 2 * width :]))
    loads["image", p].wait()
    loads["sens", p].wait()
    if p == 0:
        start_later()
    image_re = image_ref[p, 0, 0]
    image_im = image_ref[p, 0, 1]

    def sens(c):
        return sens_ref[c, p, 0].astype(jnp.float32), sens_ref[c, p, 1].astype(jnp.float32)

    lines = []
    for side in sides:
        coil_re, coil_im = [], []
        for c in side:
            sens_re, sens_im = sens(c)
            coil_re.append(sens_re * image_re - sens_im * image_im)
            coil_im.append(sens_re * image_im + sens_im * image_re)
        stacked = jnp.concatenate([jnp.concatenate(coil_re, axis=1), jnp.concatenate(coil_im, axis=1)], axis=0)
        lines.append(from_left(table_ref[0], stacked))
    into = parts_ref[pl.ds(4 * width, 2 * width)]
    out = jnp.concatenate([parts_ref[pl.ds(6 * width, width)], parts_ref[pl.ds(7 * width, width)]], axis=1)
    grad_re = jnp.zeros_like(image_re)
    grad_im = jnp.zeros_like(image_im)
    for side, line, data in zip(sides, lines, known):
        count = len(side)

        def part(k, n):
            return line[k * width : (k + 1) * width, n * width : (n + 1) * width]

        low = jnp.concatenate(
            [
                jnp.concatenate(
                    [jnp.concatenate([part(k, n)[:CENTER], part(k, n)[width - CENTER :]], axis=0) for k in range(2)],
                    axis=1,
                )
                for n in range(count)
            ],
            axis=0,
        )
        weight = jnp.concatenate([edge] * count, axis=0)
        found = mul(jnp.concatenate(halves(low), axis=0), into)
        found = found[: low.shape[0]] + found[low.shape[0] :]
        found = weight * (found + pltpu.roll(found, width - 4 * CENTER, 1))
        found_high = found.astype(jnp.bfloat16).astype(jnp.float32)
        three = found_high + pltpu.roll(found_high, 4 * CENTER, 1) + pltpu.roll(found - found_high, 8 * CENTER, 1)
        added = mul(three.astype(jnp.bfloat16), out)
        resid = ([], [])
        for n in range(count):
            both = []
            for k in range(2):
                both.append(part(k, n) + half * pltpu.roll(part(k, n), width // 2, 1))
            turned = [pltpu.roll(value, width // 4, 1) for value in both]
            sums = [
                both[0] + (real * turned[0] - imag * turned[1]),
                both[1] + (real * turned[1] + imag * turned[0]),
            ]
            for k in range(2):
                value = sums[k] - data[n * width : (n + 1) * width, k * width : (k + 1) * width]
                more = added[2 * CENTER * n : 2 * CENTER * (n + 1), k * width : (k + 1) * width]
                resid[k].append(
                    jnp.concatenate(
                        [
                            value[:CENTER] + more[:CENTER],
                            value[CENTER : width - CENTER],
                            value[width - CENTER :] + more[CENTER:],
                        ],
                        axis=0,
                    )
                )
        back = from_left(table_ref[1], jnp.concatenate([jnp.concatenate(r, axis=1) for r in resid], axis=0))
        for n, c in enumerate(side):
            back_re = back[:width, n * width : (n + 1) * width]
            back_im = back[width:, n * width : (n + 1) * width]
            sens_re, sens_im = sens(c)
            grad_re += sens_re * back_re + sens_im * back_im
            grad_im += sens_re * back_im - sens_im * back_re
    scaled = step * (1.0 / ACCEL)
    return image_re - scaled * grad_re, image_im - scaled * grad_im


def sweep(matrix, order):
    for k in range(order):
        pivot = 1.0 / matrix[k, k][0]
        column = {}
        for i in range(order):
            if i > k:
                column[i] = matrix[i, k]
            elif i < k:
                column[i] = (matrix[k, i][0], -matrix[k, i][1])
        scaled = {i: (re * pivot, im * pivot) for i, (re, im) in column.items()}
        for i in column:
            for j in column:
                if j > i:
                    continue
                a_re, a_im = scaled[i]
                b_re, b_im = column[j]
                re, im = matrix[i, j]
                re = re - (a_re * b_re + a_im * b_im)
                if i != j:
                    im = im - (a_im * b_re - a_re * b_im)
                matrix[i, j] = (re, im)
        for i in column:
            if i > k:
                matrix[i, k] = scaled[i]
            else:
                matrix[k, i] = (scaled[i][0], -scaled[i][1])
        matrix[k, k] = (-pivot, None)
    return matrix


def step_kernel(
    planes, frames, group, coils, width_y, width_z,
    step_ref, level_ref, shifts_hbm, offsets_hbm, image_hbm, sens_hbm, kspace_hbm, table_hbm,
    out_ref,
    shifts_ref, offsets_ref, image_ref, sens_ref, kspace_ref, parts_ref, table_ref, load_sem,
    wrapped, rolled, gathered, entries, inverse, finished, landed,
    send_out, recv_out, send_back, recv_back,
):
    total = frames * group
    plane_me = lax.axis_index("plane")
    frame_me = lax.axis_index("frame")
    part_me = lax.rem(plane_me, group)
    base = plane_me - part_me
    me = frame_me * group + part_me
    rows = PATCH_Y
    everyone = [(f, q) for f in range(frames) for q in range(group)]

    def other(f, q):
        return (frame_me != f) | (part_me != q)

    barrier = pltpu.get_barrier_semaphore()
    for f, q in everyone:

        @pl.when(other(f, q))
        def _():
            pl.semaphore_signal(
                barrier, inc=1, device_id={"plane": base + q, "frame": f}, device_id_type=pl.DeviceIdType.MESH
            )

    loads = {}

    def load(name, source, target):
        loads[name] = pltpu.make_async_copy(source, target, load_sem.at[len(loads)])
        loads[name].start()

    load("offsets", offsets_hbm, offsets_ref)
    load("table", table_hbm, parts_ref)

    def load_plane(p):
        load(("kspace", p), kspace_hbm.at[:, p], kspace_ref.at[:, p])
        load(("image", p), image_hbm.at[p], image_ref.at[p])
        load(("sens", p), sens_hbm.at[:, p], sens_ref.at[:, p])

    load_plane(0)
    load("shifts", shifts_hbm, shifts_ref)

    def start_later():
        for p in range(1, planes):
            load_plane(p)

    loads["offsets"].wait()
    patterns = row_patterns(offsets_ref, None, width_y, width_z)
    loads["table"].wait()
    lay_tables(parts_ref, table_ref, width_y)

    half, quarter = frames // 2, frames // 4
    far = frame_me // half
    near = 1 - far
    step_in = lax.rem(frame_me // quarter, 2)
    inner = lax.rem(frame_me, quarter)

    def order_out(token):
        zone, only = token[0], token[1:]
        z_high, z_low, maybe = {
            "a": (near, far, False), "b": (near, near, False), "c": (far, near, True), "d": (far, far, True),
            "3": (near, 1 - step_in, False), "2": (near, step_in, False), "1": (far, 1 - step_in, False), "0": (far, step_in, True),
            "W": (0, 0, True), "X": (0, 1, True), "Y": (1, 0, True), "Z": (1, 1, True),
        }[zone]
        for k in reversed(range(quarter)):
            x = lax.rem(inner + k, quarter)
            if only in ("0", "1"):
                yield z_high * half + z_low * quarter + x, int(only), maybe and k == 0
                continue
            for r in reversed(range(group)):
                q = lax.rem(part_me + r, group)
                yield z_high * half + z_low * quarter + x, q, maybe and k == 0 and r == 0

    def send(p, f, q, maybe):
        block = rolled.at[p, :, pl.ds(pl.multiple_of((f * group + q) * rows, rows), rows), :]
        copy = pltpu.make_async_remote_copy(
            src_ref=block,
            dst_ref=gathered.at[p, part_me, frame_me],
            send_sem=send_out.at[p],
            recv_sem=recv_out.at[p],
            device_id={"plane": base + q, "frame": f},
            device_id_type=pl.DeviceIdType.MESH,
        )
        if maybe:
            pl.when(other(f, q))(copy.start)
        else:
            copy.start()

    def landed_all(ref, sem):
        pltpu.make_async_copy(ref, ref, sem).wait()

    for p in range(planes):
        moved = moved_plane(loads, start_later, p, coils, width_y, image_ref, sens_ref, kspace_ref, parts_ref, table_ref, step_ref[0], patterns)
        if p == 0:
            loads["shifts"].wait()
        for k in range(2):
            part = pltpu.roll(moved[k], shifts_ref[1], 1)
            wrapped[p, k, pl.ds(0, rows), :] = part[width_y - rows :]
            wrapped[p, k, pl.ds(rows, width_y), :] = part
            rolled[p, k] = wrapped[p, k, pl.ds(rows - shifts_ref[0], width_y), :]
        if p == 0:
            pl.semaphore_wait(barrier, total - 1)
        pltpu.make_async_copy(
            rolled.at[p, :, pl.ds(pl.multiple_of(me * rows, rows), rows), :],
            gathered.at[p, part_me, frame_me],
            recv_out.at[p],
        ).start()
        for wp, zone in PLAN[p]:
            for f, q, maybe in order_out(zone):
                send(wp, f, q, maybe)

    pairs = [(f, g) for f in range(frames) for g in range(f + 1)]
    for p in range(planes):
        landed_all(gathered.at[p], recv_out.at[p])
        for n, (f, g) in enumerate(pairs):
            sum_re = None
            sum_im = None
            for q in range(group):
                f_re, f_im = gathered[p, q, f, 0], gathered[p, q, f, 1]
                g_re, g_im = gathered[p, q, g, 0], gathered[p, q, g, 1]
                re = f_re * g_re + f_im * g_im
                sum_re = re if sum_re is None else sum_re + re
                if f != g:
                    im = f_im * g_re - f_re * g_im
                    sum_im = im if sum_im is None else sum_im + im
            spot = f * frames + g
            entries[spot] = sum_re if p == 0 else entries[spot] + sum_re
            if f != g:
                spot = g * frames + f
                entries[spot] = sum_im if p == 0 else entries[spot] + sum_im

    one_row = lax.broadcasted_iota(jnp.int32, (width_z, width_z), 0) // PATCH_Z
    one_lane = lax.broadcasted_iota(jnp.int32, (width_z, width_z), 1) // PATCH_Z
    same = (one_row == one_lane).astype(jnp.bfloat16)
    cells = entries[...]
    shift = rows // 2
    while shift:
        cells = cells + pltpu.roll(cells, shift, 1)
        shift //= 2
    high, low = halves(cells.reshape(frames * frames * rows, width_z))
    entries[...] = (mul(high, same) + mul(low, same)).reshape(frames * frames, rows, width_z)

    level = level_ref[0]
    matrix = {}
    for f, g in pairs:
        if f == g:
            matrix[f, f] = (entries[f * frames + f] + level, None)
        else:
            matrix[f, g] = (entries[f * frames + g], entries[g * frames + f])
    matrix = sweep(matrix, frames)
    for f, g in pairs:
        re, im = matrix[f, g]
        inverse[f, g, 0] = re * level
        if f != g:
            inverse[f, g, 1] = im * level
            inverse[g, f, 0] = re * level
            inverse[g, f, 1] = -im * level
        else:
            inverse[f, f, 1] = jnp.zeros_like(re)

    spot = pl.ds(pl.multiple_of(me * rows, rows), rows)
    for f in [0,6,1,7,2,4,3,5]:
        weights = [(inverse[f, g, 0], inverse[f, g, 1]) for g in range(frames)]
        for q in range(group):
            for p in range(planes):
                re = gathered[p, q, f, 0]
                im = gathered[p, q, f, 1]
                for g in range(frames):
                    g_re, g_im = gathered[p, q, g, 0], gathered[p, q, g, 1]
                    w_re, w_im = weights[g]
                    re = re + (w_re * g_re - w_im * g_im)
                    im = im + (w_re * g_im + w_im * g_re)
                finished[q, f, p, 0] = re
                finished[q, f, p, 1] = im
            place = landed.at[:, :, spot, :]
            apart = other(f, q)
            copy = pltpu.make_async_remote_copy(
                src_ref=finished.at[q, f],
                dst_ref=place,
                send_sem=send_back,
                recv_sem=recv_back,
                device_id={"plane": base + q, "frame": f},
                device_id_type=pl.DeviceIdType.MESH,
            )
            pl.when(apart)(copy.start)
            pl.when(jnp.logical_not(apart))(pltpu.make_async_copy(finished.at[q, f], place, recv_back).start)
    sent = pl.ds(0, (total - 1) * rows)
    for p in range(planes):
        landed_all(rolled.at[p, :, sent, :], send_out.at[p])
    landed_all(landed, recv_back)
    shift_z = lax.rem(width_z - shifts_ref[1], width_z)
    for p in range(planes):
        for k in range(2):
            part = pltpu.roll(landed[p, k], shift_z, 1)
            wrapped[p, k, pl.ds(0, width_y), :] = part
            wrapped[p, k, pl.ds(width_y, rows), :] = part[:rows]
            out_ref[p, 0, k] = wrapped[p, k, pl.ds(shifts_ref[0], width_y), :]
    landed_all(landed.at[:, :, sent, :], send_back)


def local_fused(image, sens, kspace, offsets, shifts, step_size, threshold):
    planes, _, _, width_y, width_z = image.shape
    coils = sens.shape[0]
    frames = lax.axis_size("frame")
    group = PATCH_X // planes
    total = frames * group
    table = jnp.asarray(block_tables(width_y))
    vmem = pl.BlockSpec(memory_space=pltpu.VMEM)
    smem = pl.BlockSpec(memory_space=pltpu.SMEM)
    hbm = pl.BlockSpec(memory_space=pltpu.HBM)
    slab = (PATCH_Y, width_z)
    dma = pltpu.SemaphoreType.DMA
    in_hbm = [
        pltpu.with_memory_space_constraint(x, pltpu.HBM) for x in (shifts, offsets, image, sens, kspace, table)
    ]
    return pl.pallas_call(
        functools.partial(step_kernel, planes, frames, group, coils, width_y, width_z),
        out_shape=jax.ShapeDtypeStruct(image.shape, jnp.float32),
        in_specs=[smem, smem] + [hbm] * 6,
        out_specs=vmem,
        scratch_shapes=[
            pltpu.SMEM(shifts.shape, shifts.dtype),
            pltpu.VMEM(offsets.shape, offsets.dtype),
            pltpu.VMEM(image.shape, image.dtype),
            pltpu.VMEM(sens.shape, sens.dtype),
            pltpu.VMEM(kspace.shape, kspace.dtype),
            pltpu.VMEM(table.shape, table.dtype),
            pltpu.VMEM((2, 4 * width_y, 2 * width_y), table.dtype),
            dma((3 * planes + 3,)),
            pltpu.VMEM((planes, 2, width_y + PATCH_Y, width_z), jnp.float32),
            pltpu.VMEM((planes, 2, width_y, width_z), jnp.float32),
            pltpu.VMEM((planes, group, frames, 2) + slab, jnp.float32),
            pltpu.VMEM((frames * frames,) + slab, jnp.float32),
            pltpu.VMEM((frames, frames, 2) + slab, jnp.float32),
            pltpu.VMEM((group, frames, planes, 2) + slab, jnp.float32),
            pltpu.VMEM((planes, 2, width_y, width_z), jnp.float32),
            dma((planes,)),
            dma((planes,)),
            dma(()),
            dma(()),
        ],
        compiler_params=pltpu.CompilerParams(collective_id=0, has_side_effects=True, vmem_limit_bytes=VMEM_BYTES),
        name="prox_step",
    )(step_size, threshold, *in_hbm)


def local(image, sens, kspace, offsets, shifts, step_size, threshold):
    planes, frames_dev, _, width_y, width_z = image.shape
    frames = frames_dev * lax.axis_size("frame")
    group = PATCH_X // planes
    one_block = frames * group * PATCH_Y == width_y and frames_dev == 1 and frames & (frames - 1) == 0
    split = group > 1 and group & (group - 1) == 0 and lax.axis_size("plane") % group == 0
    if one_block and split and width_y == width_z and width_z % 128 == 0:
        return local_fused(image, sens, kspace, offsets, shifts, step_size, threshold)
    return local_general(image, sens, kspace, offsets, shifts, step_size, threshold)


def solution(mesh):
    in_specs = (
        P("plane", "frame", None, None, None),
        P(None, "plane", None, None, None),
        P(None, "plane", "frame", None, None, None),
        P("frame", None),
        P(),
        P(),
        P(),
    )
    out_specs = P("plane", "frame", None, None, None)
    return jax.shard_map(local, mesh=mesh, in_specs=in_specs, out_specs=out_specs, check_vma=False)
```

```python
import functools
import math

import jax
import jax.numpy as jnp
import numpy as np
from jax import lax
from jax.experimental import pallas as pl
from jax.experimental.pallas import tpu as pltpu
from jax.sharding import PartitionSpec as P

PATCH_X = 4
PATCH_Y = 8
PATCH_Z = 8
ACCEL = 4
CENTER = 8
PAIR = 2


def from_partner(block, axis, distance):
    count = lax.axis_size(axis)
    route = []
    for low in range(count):
        high = low | 1 << distance
        if high != low and high < count:
            route += [(low, high), (high, low)]
    return lax.ppermute(block, axis, route)


def dft_tables(length):
    indices = jnp.arange(length, dtype=jnp.int32)
    phases = indices[:, None] * indices[None, :] % length
    angles = phases.astype(jnp.float32) * (2.0 * math.pi / length)
    norm_scale = 1.0 / math.sqrt(length)
    return (jnp.cos(angles) * norm_scale, jnp.sin(angles) * norm_scale)


def along_z(stacked, right_table, sign, width_z):
    product = jnp.einsum(
        "...z,zw->...w",
        stacked,
        right_table,
        precision=lax.Precision.HIGHEST,
        preferred_element_type=jnp.float32,
    )
    cos_part = product[..., :width_z]
    sin_part = product[..., width_z:]
    real_part = cos_part[..., 0, :, :] + sign * sin_part[..., 1, :, :]
    imag_part = cos_part[..., 1, :, :] - sign * sin_part[..., 0, :, :]
    return jnp.stack([real_part, imag_part], axis=-3)


def along_y(stacked, left_table):
    shape_in = stacked.shape
    merged = stacked.reshape(shape_in[:-3] + (2 * shape_in[-2], shape_in[-1]))
    result = jnp.einsum(
        "ur,...rz->...uz",
        left_table,
        merged,
        precision=lax.Precision.HIGHEST,
        preferred_element_type=jnp.float32,
    )
    return result.reshape(shape_in)


def rotate(casorati):
    frames2, voxels = (casorati.shape[-2], casorati.shape[-1])
    split_parts = casorati.reshape(casorati.shape[:-2] + (frames2 // 2, 2, voxels))
    turned = jnp.stack([-split_parts[..., 1, :], split_parts[..., 0, :]], axis=-2)
    return turned.reshape(casorati.shape)


def gram_of(casorati):
    twin = rotate(casorati)
    first = jnp.einsum(
        "kav,kbv->kab",
        casorati,
        casorati,
        precision=lax.Precision.HIGHEST,
        preferred_element_type=jnp.float32,
    )
    second = jnp.einsum(
        "kav,kbv->kab",
        twin,
        twin,
        precision=lax.Precision.HIGHEST,
        preferred_element_type=jnp.float32,
    )
    return first + second


def shrink(casorati, gram, level):
    order = gram.shape[-1]
    system = gram + level * jnp.eye(order, dtype=jnp.float32)
    factor = jnp.linalg.cholesky(system)
    forward_part = jax.scipy.linalg.solve_triangular(factor, casorati, lower=True)
    solved = jax.scipy.linalg.solve_triangular(factor, forward_part, lower=True, trans=1)
    return casorati - level * solved


def local_general(image, sens, kspace, offsets, shifts, step_size, threshold):
    planes, frames_dev, _, width_y, width_z = image.shape
    frames = frames_dev * lax.axis_size("frame")
    cos_y, sin_y = dft_tables(width_y)
    cos_z, sin_z = dft_tables(width_z)
    right_table = jnp.concatenate([cos_z, sin_z], axis=1)
    left_forward = jnp.concatenate(
        [jnp.concatenate([cos_y, sin_y], axis=1), jnp.concatenate([-sin_y, cos_y], axis=1)], axis=0
    )
    left_inverse = jnp.concatenate(
        [jnp.concatenate([cos_y, -sin_y], axis=1), jnp.concatenate([sin_y, cos_y], axis=1)], axis=0
    )
    rows_y = jnp.arange(width_y, dtype=jnp.int32)
    rows_z = jnp.arange(width_z, dtype=jnp.int32)
    low_y = (rows_y < CENTER) | (rows_y >= width_y - CENTER)
    low_z = (rows_z < CENTER) | (rows_z >= width_z - CENTER)
    regular = (rows_z[None, None, :] + offsets[:, :, None]) % ACCEL == 0
    sampled = (regular | low_y[None, :, None] & low_z[None, None, :]).astype(jnp.float32)
    image_re = image[:, :, 0]
    image_im = image[:, :, 1]
    maps = sens.astype(jnp.float32)
    sens_re = maps[:, :, 0][:, :, None]
    sens_im = maps[:, :, 1][:, :, None]
    coil_re = sens_re * image_re[None] - sens_im * image_im[None]
    coil_im = sens_re * image_im[None] + sens_im * image_re[None]
    stacked = jnp.stack([coil_re, coil_im], axis=3)
    spectra = along_y(along_z(stacked, right_table, 1.0, width_z), left_forward)
    resid = sampled[None, None, :, None] * (spectra - kspace.astype(jnp.float32))
    returned = along_z(along_y(resid, left_inverse), right_table, -1.0, width_z)
    back_re = returned[:, :, :, 0]
    back_im = returned[:, :, :, 1]
    grad_re = jnp.sum(sens_re * back_re + sens_im * back_im, axis=0)
    grad_im = jnp.sum(sens_re * back_im - sens_im * back_re, axis=0)
    moved = image - step_size[0] * jnp.stack([grad_re, grad_im], axis=2)
    rolled = jnp.roll(moved, (shifts[0], shifts[1]), axis=(3, 4))
    nyb = width_y // PATCH_Y
    nzb = width_z // PATCH_Z
    voxels = planes * PATCH_Y * PATCH_Z
    blocks = rolled.reshape(planes, frames_dev, 2, nyb, PATCH_Y, nzb, PATCH_Z)
    blocks = blocks.transpose(3, 5, 1, 2, 0, 4, 6).reshape(nyb * nzb, frames_dev, 2, voxels)
    regrouped = lax.all_to_all(blocks, "frame", split_axis=0, concat_axis=1, tiled=True)
    count = regrouped.shape[0]
    casorati = regrouped.reshape(count, 2 * frames, voxels)
    level = threshold[0]
    parity = lax.axis_index("plane") % 2
    halfway = count // 2
    first_part = casorati[:halfway]
    second_part = casorati[halfway:]
    kept_part = jnp.where(parity == 0, first_part, second_part)
    outgoing = jnp.where(parity == 0, second_part, first_part)
    incoming = from_partner(outgoing, "plane", 0)
    complete = jnp.concatenate([kept_part, incoming], axis=2)
    finished = shrink(complete, gram_of(complete), level)
    own_part = finished[:, :, :voxels]
    returned_part = from_partner(finished[:, :, voxels:], "plane", 0)
    shrunk = jnp.where(
        parity == 0,
        jnp.concatenate([own_part, returned_part], axis=0),
        jnp.concatenate([returned_part, own_part], axis=0),
    )
    restored = lax.all_to_all(
        shrunk.reshape(count, frames, 2, voxels), "frame", split_axis=1, concat_axis=0, tiled=True
    )
    placed = restored.reshape(nyb, nzb, frames_dev, 2, planes, PATCH_Y, PATCH_Z)
    placed = placed.transpose(4, 2, 3, 0, 5, 1, 6).reshape(planes, frames_dev, 2, width_y, width_z)
    return jnp.roll(placed, (-shifts[0], -shifts[1]), axis=(3, 4))


VMEM_BYTES = 24 * 1024 * 1024


PLAN = [[(0, 'W'), (0, 'Y'), (0, 'X'), (0, 'Z')], [(1, 'W'), (1, 'Y'), (1, 'X'), (1, 'Z')]]


def two_parts(table):
    high = table.astype(jnp.bfloat16)
    return high, (table - high.astype(np.float64)).astype(jnp.bfloat16)


def block_tables(length):
    indices = np.arange(length)
    angles = (indices[:, None] * indices[None, :] % length) * (2.0 * np.pi / length)
    cos = np.cos(angles) / np.sqrt(length)
    sin = np.sin(angles) / np.sqrt(length)
    centre = np.concatenate([indices[:CENTER], indices[length - CENTER :]])
    into = np.block([[cos, -sin], [sin, cos]])[:, np.concatenate([centre, length + centre])]
    into_high, into_low = two_parts(into)
    from_high, from_low = two_parts(into.T)
    rest = length - 4 * len(centre)
    into = np.concatenate([into_high, into_low, np.zeros((2 * length, rest), jnp.bfloat16)], axis=1)
    rest = length - 6 * len(centre)
    back = np.concatenate([from_high, from_low, from_high, np.zeros((rest, 2 * length), jnp.bfloat16)], axis=0)
    whole = np.concatenate([*two_parts(cos), *two_parts(sin)], axis=0)
    return np.concatenate([whole, into, back[:, :length], back[:, length:]], axis=0)


def lay_tables(parts_ref, table_ref, width):
    low, top = pl.ds(0, width), pl.ds(width, width)
    for k in range(2):
        cos, sin = parts_ref[pl.ds(k * width, width)], parts_ref[pl.ds((2 + k) * width, width)]
        for table, upper, lower in ((0, sin, -sin), (1, -sin, sin)):
            first, second = pl.ds(2 * k * width, width), pl.ds((2 * k + 1) * width, width)
            table_ref[table, first, low] = cos
            table_ref[table, second, top] = cos
            table_ref[table, first, top] = upper
            table_ref[table, second, low] = lower


def halves(values):
    high = values.astype(jnp.bfloat16)
    return high, (values - high.astype(jnp.float32)).astype(jnp.bfloat16)


def mul(left, right):
    return jnp.dot(left, right, preferred_element_type=jnp.float32)


def from_left(table, values):
    count = table.shape[1]
    value_high, value_low = halves(values)
    first = mul(table, value_high)
    return first[:count] + (first[count:] + mul(table[:count], value_low))


def row_patterns(offsets_ref, offset_rows, width_y, width_z):
    lane = lax.broadcasted_iota(jnp.int32, (width_y, width_z), 1)
    row = lax.broadcasted_iota(jnp.int32, (width_y, width_z), 0)
    offset = jnp.broadcast_to(offsets_ref[...].astype(jnp.float32), (width_z, width_y)).T
    wanted = jnp.where(offset == 0.0, 0.0, ACCEL - offset)
    regular = lax.rem(lane, ACCEL).astype(jnp.float32) == wanted
    low_y = (row < CENTER) | (row >= width_y - CENTER)
    low_z = (lane < CENTER) | (lane >= width_z - CENTER)
    centre = low_y & low_z
    scale = float(ACCEL)
    kept = jnp.where(regular | centre, scale, 0.0).astype(jnp.bfloat16)
    extra = jnp.where(centre & jnp.logical_not(regular), scale, 0.0)
    edge = jnp.concatenate([extra[:CENTER], extra[width_y - CENTER :]], axis=0)
    edge = jnp.where(lane[: 2 * CENTER] < CENTER, edge, pltpu.roll(edge, 2 * CENTER, 1))
    slot = lane[: 2 * CENTER]
    edge = jnp.where(slot < 2 * CENTER, edge, jnp.where(slot < 4 * CENTER, pltpu.roll(edge, 2 * CENTER, 1), 0.0))
    half = jnp.where((offset == 0.0) | (offset == 2.0), 1.0, -1.0)
    real = jnp.where(offset == 0.0, 1.0, jnp.where(offset == 2.0, -1.0, 0.0))
    imag = jnp.where(offset == 1.0, -1.0, jnp.where(offset == 3.0, 1.0, 0.0))
    return kept, edge, half, real, imag


def moved_plane(loads, start_later, p, coils, width, image_ref, sens_ref, kspace_ref, parts_ref, table_ref, step, patterns):
    kept, edge, half, real, imag = patterns
    sides = [range(c, min(c + PAIR, coils)) for c in range(0, coils, PAIR)]
    loads["kspace", p].wait()
    known = []
    for side in sides:
        data = jnp.concatenate(
            [jnp.concatenate([kspace_ref[c, p, 0, k] * kept for k in range(2)], axis=1) for c in side], axis=0
        )
        known.append(mul(data, table_ref[0, : 2 * width]) + mul(data, table_ref[0, 2 * width :]))
    loads["image", p].wait()
    loads["sens", p].wait()
    if p == 0:
        start_later()
    image_re = image_ref[p, 0, 0]
    image_im = image_ref[p, 0, 1]

    def sens(c):
        return sens_ref[c, p, 0].astype(jnp.float32), sens_ref[c, p, 1].astype(jnp.float32)

    lines = []
    for side in sides:
        coil_re, coil_im = [], []
        for c in side:
            sens_re, sens_im = sens(c)
            coil_re.append(sens_re * image_re - sens_im * image_im)
            coil_im.append(sens_re * image_im + sens_im * image_re)
        stacked = jnp.concatenate([jnp.concatenate(coil_re, axis=1), jnp.concatenate(coil_im, axis=1)], axis=0)
        lines.append(from_left(table_ref[0], stacked))
    into = parts_ref[pl.ds(4 * width, 2 * width)]
    out = jnp.concatenate([parts_ref[pl.ds(6 * width, width)], parts_ref[pl.ds(7 * width, width)]], axis=1)
    grad_re = jnp.zeros_like(image_re)
    grad_im = jnp.zeros_like(image_im)
    for side, line, data in zip(sides, lines, known):
        count = len(side)

        def part(k, n):
            return line[k * width : (k + 1) * width, n * width : (n + 1) * width]

        low = jnp.concatenate(
            [
                jnp.concatenate(
                    [jnp.concatenate([part(k, n)[:CENTER], part(k, n)[width - CENTER :]], axis=0) for k in range(2)],
                    axis=1,
                )
                for n in range(count)
            ],
            axis=0,
        )
        weight = jnp.concatenate([edge] * count, axis=0)
        found = mul(jnp.concatenate(halves(low), axis=0), into)
        found = found[: low.shape[0]] + found[low.shape[0] :]
        found = weight * (found + pltpu.roll(found, width - 4 * CENTER, 1))
        found_high = found.astype(jnp.bfloat16).astype(jnp.float32)
        three = found_high + pltpu.roll(found_high, 4 * CENTER, 1) + pltpu.roll(found - found_high, 8 * CENTER, 1)
        added = mul(three.astype(jnp.bfloat16), out)
        resid = ([], [])
        for n in range(count):
            both = []
            for k in range(2):
                both.append(part(k, n) + half * pltpu.roll(part(k, n), width // 2, 1))
            turned = [pltpu.roll(value, width // 4, 1) for value in both]
            sums = [
                both[0] + (real * turned[0] - imag * turned[1]),
                both[1] + (real * turned[1] + imag * turned[0]),
            ]
            for k in range(2):
                value = sums[k] - data[n * width : (n + 1) * width, k * width : (k + 1) * width]
                more = added[2 * CENTER * n : 2 * CENTER * (n + 1), k * width : (k + 1) * width]
                resid[k].append(
                    jnp.concatenate(
                        [
                            value[:CENTER] + more[:CENTER],
                            value[CENTER : width - CENTER],
                            value[width - CENTER :] + more[CENTER:],
                        ],
                        axis=0,
                    )
                )
        back = from_left(table_ref[1], jnp.concatenate([jnp.concatenate(r, axis=1) for r in resid], axis=0))
        for n, c in enumerate(side):
            back_re = back[:width, n * width : (n + 1) * width]
            back_im = back[width:, n * width : (n + 1) * width]
            sens_re, sens_im = sens(c)
            grad_re += sens_re * back_re + sens_im * back_im
            grad_im += sens_re * back_im - sens_im * back_re
    scaled = step * (1.0 / ACCEL)
    return image_re - scaled * grad_re, image_im - scaled * grad_im


def sweep(matrix, order):
    for k in range(order):
        pivot = 1.0 / matrix[k, k][0]
        column = {}
        for i in range(order):
            if i > k:
                column[i] = matrix[i, k]
            elif i < k:
                column[i] = (matrix[k, i][0], -matrix[k, i][1])
        scaled = {i: (re * pivot, im * pivot) for i, (re, im) in column.items()}
        for i in column:
            for j in column:
                if j > i:
                    continue
                a_re, a_im = scaled[i]
                b_re, b_im = column[j]
                re, im = matrix[i, j]
                re = re - (a_re * b_re + a_im * b_im)
                if i != j:
                    im = im - (a_im * b_re - a_re * b_im)
                matrix[i, j] = (re, im)
        for i in column:
            if i > k:
                matrix[i, k] = scaled[i]
            else:
                matrix[k, i] = (scaled[i][0], -scaled[i][1])
        matrix[k, k] = (-pivot, None)
    return matrix


def step_kernel(
    planes, frames, group, coils, width_y, width_z,
    step_ref, level_ref, shifts_hbm, offsets_hbm, image_hbm, sens_hbm, kspace_hbm, table_hbm,
    out_ref,
    shifts_ref, offsets_ref, image_ref, sens_ref, kspace_ref, parts_ref, table_ref, load_sem,
    wrapped, rolled, gathered, entries, inverse, finished, landed,
    send_out, recv_out, send_back, recv_back,
):
    total = frames * group
    plane_me = lax.axis_index("plane")
    frame_me = lax.axis_index("frame")
    part_me = lax.rem(plane_me, group)
    base = plane_me - part_me
    me = frame_me * group + part_me
    rows = PATCH_Y
    everyone = [(f, q) for f in range(frames) for q in range(group)]

    def other(f, q):
        return (frame_me != f) | (part_me != q)

    barrier = pltpu.get_barrier_semaphore()
    for f, q in everyone:

        @pl.when(other(f, q))
        def _():
            pl.semaphore_signal(
                barrier, inc=1, device_id={"plane": base + q, "frame": f}, device_id_type=pl.DeviceIdType.MESH
            )

    loads = {}

    def load(name, source, target):
        loads[name] = pltpu.make_async_copy(source, target, load_sem.at[len(loads)])
        loads[name].start()

    load("offsets", offsets_hbm, offsets_ref)
    load("table", table_hbm, parts_ref)

    def load_plane(p):
        load(("kspace", p), kspace_hbm.at[:, p], kspace_ref.at[:, p])
        load(("image", p), image_hbm.at[p], image_ref.at[p])
        load(("sens", p), sens_hbm.at[:, p], sens_ref.at[:, p])

    load_plane(0)
    load("shifts", shifts_hbm, shifts_ref)

    def start_later():
        for p in range(1, planes):
            load_plane(p)

    loads["offsets"].wait()
    patterns = row_patterns(offsets_ref, None, width_y, width_z)
    loads["table"].wait()
    lay_tables(parts_ref, table_ref, width_y)

    half, quarter = frames // 2, frames // 4
    far = frame_me // half
    near = 1 - far
    step_in = lax.rem(frame_me // quarter, 2)
    inner = lax.rem(frame_me, quarter)

    def order_out(token):
        zone, only = token[0], token[1:]
        z_high, z_low, maybe = {
            "a": (near, far, False), "b": (near, near, False), "c": (far, near, True), "d": (far, far, True),
            "3": (near, 1 - step_in, False), "2": (near, step_in, False), "1": (far, 1 - step_in, False), "0": (far, step_in, True),
            "W": (0, 0, True), "X": (0, 1, True), "Y": (1, 0, True), "Z": (1, 1, True),
        }[zone]
        for k in reversed(range(quarter)):
            x = lax.rem(inner + k, quarter)
            if only in ("0", "1"):
                yield z_high * half + z_low * quarter + x, int(only), maybe and k == 0
                continue
            for r in reversed(range(group)):
                q = lax.rem(part_me + r, group)
                yield z_high * half + z_low * quarter + x, q, maybe and k == 0 and r == 0

    def send(p, f, q, maybe):
        block = rolled.at[p, :, pl.ds(pl.multiple_of((f * group + q) * rows, rows), rows), :]
        copy = pltpu.make_async_remote_copy(
            src_ref=block,
            dst_ref=gathered.at[p, part_me, frame_me],
            send_sem=send_out.at[p],
            recv_sem=recv_out.at[p],
            device_id={"plane": base + q, "frame": f},
            device_id_type=pl.DeviceIdType.MESH,
        )
        if maybe:
            pl.when(other(f, q))(copy.start)
        else:
            copy.start()

    def landed_all(ref, sem):
        pltpu.make_async_copy(ref, ref, sem).wait()

    for p in range(planes):
        moved = moved_plane(loads, start_later, p, coils, width_y, image_ref, sens_ref, kspace_ref, parts_ref, table_ref, step_ref[0], patterns)
        if p == 0:
            loads["shifts"].wait()
        for k in range(2):
            part = pltpu.roll(moved[k], shifts_ref[1], 1)
            wrapped[p, k, pl.ds(0, rows), :] = part[width_y - rows :]
            wrapped[p, k, pl.ds(rows, width_y), :] = part
            rolled[p, k] = wrapped[p, k, pl.ds(rows - shifts_ref[0], width_y), :]
        if p == 0:
            pl.semaphore_wait(barrier, total - 1)
        pltpu.make_async_copy(
            rolled.at[p, :, pl.ds(pl.multiple_of(me * rows, rows), rows), :],
            gathered.at[p, part_me, frame_me],
            recv_out.at[p],
        ).start()
        for wp, zone in PLAN[p]:
            for f, q, maybe in order_out(zone):
                send(wp, f, q, maybe)

    pairs = [(f, g) for f in range(frames) for g in range(f + 1)]
    for p in range(planes):
        landed_all(gathered.at[p], recv_out.at[p])
        for n, (f, g) in enumerate(pairs):
            sum_re = None
            sum_im = None
            for q in range(group):
                f_re, f_im = gathered[p, q, f, 0], gathered[p, q, f, 1]
                g_re, g_im = gathered[p, q, g, 0], gathered[p, q, g, 1]
                re = f_re * g_re + f_im * g_im
                sum_re = re if sum_re is None else sum_re + re
                if f != g:
                    im = f_im * g_re - f_re * g_im
                    sum_im = im if sum_im is None else sum_im + im
            spot = f * frames + g
            entries[spot] = sum_re if p == 0 else entries[spot] + sum_re
            if f != g:
                spot = g * frames + f
                entries[spot] = sum_im if p == 0 else entries[spot] + sum_im

    one_row = lax.broadcasted_iota(jnp.int32, (width_z, width_z), 0) // PATCH_Z
    one_lane = lax.broadcasted_iota(jnp.int32, (width_z, width_z), 1) // PATCH_Z
    same = (one_row == one_lane).astype(jnp.bfloat16)
    cells = entries[...]
    shift = rows // 2
    while shift:
        cells = cells + pltpu.roll(cells, shift, 1)
        shift //= 2
    high, low = halves(cells.reshape(frames * frames * rows, width_z))
    entries[...] = (mul(high, same) + mul(low, same)).reshape(frames * frames, rows, width_z)

    level = level_ref[0]
    matrix = {}
    for f, g in pairs:
        if f == g:
            matrix[f, f] = (entries[f * frames + f] + level, None)
        else:
            matrix[f, g] = (entries[f * frames + g], entries[g * frames + f])
    matrix = sweep(matrix, frames)
    for f, g in pairs:
        re, im = matrix[f, g]
        inverse[f, g, 0] = re * level
        if f != g:
            inverse[f, g, 1] = im * level
            inverse[g, f, 0] = re * level
            inverse[g, f, 1] = -im * level
        else:
            inverse[f, f, 1] = jnp.zeros_like(re)

    spot = pl.ds(pl.multiple_of(me * rows, rows), rows)
    for f in [0, 6, 1, 4, 2, 3, 7, 5]:
        weights = [(inverse[f, g, 0], inverse[f, g, 1]) for g in range(frames)]
        for q in range(group):
            for p in range(planes):
                re = gathered[p, q, f, 0]
                im = gathered[p, q, f, 1]
                for g in range(frames):
                    g_re, g_im = gathered[p, q, g, 0], gathered[p, q, g, 1]
                    w_re, w_im = weights[g]
                    re = re + (w_re * g_re - w_im * g_im)
                    im = im + (w_re * g_im + w_im * g_re)
                finished[q, f, p, 0] = re
                finished[q, f, p, 1] = im
            place = landed.at[:, :, spot, :]
            apart = other(f, q)
            copy = pltpu.make_async_remote_copy(
                src_ref=finished.at[q, f],
                dst_ref=place,
                send_sem=send_back,
                recv_sem=recv_back,
                device_id={"plane": base + q, "frame": f},
                device_id_type=pl.DeviceIdType.MESH,
            )
            pl.when(apart)(copy.start)
            pl.when(jnp.logical_not(apart))(pltpu.make_async_copy(finished.at[q, f], place, recv_back).start)
    sent = pl.ds(0, (total - 1) * rows)
    for p in range(planes):
        landed_all(rolled.at[p, :, sent, :], send_out.at[p])
    landed_all(landed, recv_back)
    shift_z = lax.rem(width_z - shifts_ref[1], width_z)
    for p in range(planes):
        for k in range(2):
            part = pltpu.roll(landed[p, k], shift_z, 1)
            wrapped[p, k, pl.ds(0, width_y), :] = part
            wrapped[p, k, pl.ds(width_y, rows), :] = part[:rows]
            out_ref[p, 0, k] = wrapped[p, k, pl.ds(shifts_ref[0], width_y), :]
    landed_all(landed.at[:, :, sent, :], send_back)


def local_fused(image, sens, kspace, offsets, shifts, step_size, threshold):
    planes, _, _, width_y, width_z = image.shape
    coils = sens.shape[0]
    frames = lax.axis_size("frame")
    group = PATCH_X // planes
    total = frames * group
    table = jnp.asarray(block_tables(width_y))
    vmem = pl.BlockSpec(memory_space=pltpu.VMEM)
    smem = pl.BlockSpec(memory_space=pltpu.SMEM)
    hbm = pl.BlockSpec(memory_space=pltpu.HBM)
    slab = (PATCH_Y, width_z)
    dma = pltpu.SemaphoreType.DMA
    in_hbm = [
        pltpu.with_memory_space_constraint(x, pltpu.HBM) for x in (shifts, offsets, image, sens, kspace, table)
    ]
    return pl.pallas_call(
        functools.partial(step_kernel, planes, frames, group, coils, width_y, width_z),
        out_shape=jax.ShapeDtypeStruct(image.shape, jnp.float32),
        in_specs=[smem, smem] + [hbm] * 6,
        out_specs=vmem,
        scratch_shapes=[
            pltpu.SMEM(shifts.shape, shifts.dtype),
            pltpu.VMEM(offsets.shape, offsets.dtype),
            pltpu.VMEM(image.shape, image.dtype),
            pltpu.VMEM(sens.shape, sens.dtype),
            pltpu.VMEM(kspace.shape, kspace.dtype),
            pltpu.VMEM(table.shape, table.dtype),
            pltpu.VMEM((2, 4 * width_y, 2 * width_y), table.dtype),
            dma((3 * planes + 3,)),
            pltpu.VMEM((planes, 2, width_y + PATCH_Y, width_z), jnp.float32),
            pltpu.VMEM((planes, 2, width_y, width_z), jnp.float32),
            pltpu.VMEM((planes, group, frames, 2) + slab, jnp.float32),
            pltpu.VMEM((frames * frames,) + slab, jnp.float32),
            pltpu.VMEM((frames, frames, 2) + slab, jnp.float32),
            pltpu.VMEM((group, frames, planes, 2) + slab, jnp.float32),
            pltpu.VMEM((planes, 2, width_y, width_z), jnp.float32),
            dma((planes,)),
            dma((planes,)),
            dma(()),
            dma(()),
        ],
        compiler_params=pltpu.CompilerParams(collective_id=0, has_side_effects=True, vmem_limit_bytes=VMEM_BYTES),
        name="prox_step",
    )(step_size, threshold, *in_hbm)


def local(image, sens, kspace, offsets, shifts, step_size, threshold):
    planes, frames_dev, _, width_y, width_z = image.shape
    frames = frames_dev * lax.axis_size("frame")
    group = PATCH_X // planes
    one_block = frames * group * PATCH_Y == width_y and frames_dev == 1 and frames & (frames - 1) == 0
    split = group > 1 and group & (group - 1) == 0 and lax.axis_size("plane") % group == 0
    if one_block and split and width_y == width_z and width_z % 128 == 0:
        return local_fused(image, sens, kspace, offsets, shifts, step_size, threshold)
    return local_general(image, sens, kspace, offsets, shifts, step_size, threshold)


def solution(mesh):
    in_specs = (
        P("plane", "frame", None, None, None),
        P(None, "plane", None, None, None),
        P(None, "plane", "frame", None, None, None),
        P("frame", None),
        P(),
        P(),
        P(),
    )
    out_specs = P("plane", "frame", None, None, None)
    return jax.shard_map(local, mesh=mesh, in_specs=in_specs, out_specs=out_specs, check_vma=False)
```

```python
import functools
import math

import jax
import jax.numpy as jnp
import numpy as np
from jax import lax
from jax.experimental import pallas as pl
from jax.experimental.pallas import tpu as pltpu
from jax.sharding import PartitionSpec as P

PATCH_X = 4
PATCH_Y = 8
PATCH_Z = 8
ACCEL = 4
CENTER = 8
PAIR = 2


def from_partner(block, axis, distance):
    count = lax.axis_size(axis)
    route = []
    for low in range(count):
        high = low | 1 << distance
        if high != low and high < count:
            route += [(low, high), (high, low)]
    return lax.ppermute(block, axis, route)


def dft_tables(length):
    indices = jnp.arange(length, dtype=jnp.int32)
    phases = indices[:, None] * indices[None, :] % length
    angles = phases.astype(jnp.float32) * (2.0 * math.pi / length)
    norm_scale = 1.0 / math.sqrt(length)
    return (jnp.cos(angles) * norm_scale, jnp.sin(angles) * norm_scale)


def along_z(stacked, right_table, sign, width_z):
    product = jnp.einsum(
        "...z,zw->...w",
        stacked,
        right_table,
        precision=lax.Precision.HIGHEST,
        preferred_element_type=jnp.float32,
    )
    cos_part = product[..., :width_z]
    sin_part = product[..., width_z:]
    real_part = cos_part[..., 0, :, :] + sign * sin_part[..., 1, :, :]
    imag_part = cos_part[..., 1, :, :] - sign * sin_part[..., 0, :, :]
    return jnp.stack([real_part, imag_part], axis=-3)


def along_y(stacked, left_table):
    shape_in = stacked.shape
    merged = stacked.reshape(shape_in[:-3] + (2 * shape_in[-2], shape_in[-1]))
    result = jnp.einsum(
        "ur,...rz->...uz",
        left_table,
        merged,
        precision=lax.Precision.HIGHEST,
        preferred_element_type=jnp.float32,
    )
    return result.reshape(shape_in)


def rotate(casorati):
    frames2, voxels = (casorati.shape[-2], casorati.shape[-1])
    split_parts = casorati.reshape(casorati.shape[:-2] + (frames2 // 2, 2, voxels))
    turned = jnp.stack([-split_parts[..., 1, :], split_parts[..., 0, :]], axis=-2)
    return turned.reshape(casorati.shape)


def gram_of(casorati):
    twin = rotate(casorati)
    first = jnp.einsum(
        "kav,kbv->kab",
        casorati,
        casorati,
        precision=lax.Precision.HIGHEST,
        preferred_element_type=jnp.float32,
    )
    second = jnp.einsum(
        "kav,kbv->kab",
        twin,
        twin,
        precision=lax.Precision.HIGHEST,
        preferred_element_type=jnp.float32,
    )
    return first + second


def shrink(casorati, gram, level):
    order = gram.shape[-1]
    system = gram + level * jnp.eye(order, dtype=jnp.float32)
    factor = jnp.linalg.cholesky(system)
    forward_part = jax.scipy.linalg.solve_triangular(factor, casorati, lower=True)
    solved = jax.scipy.linalg.solve_triangular(factor, forward_part, lower=True, trans=1)
    return casorati - level * solved


def local_general(image, sens, kspace, offsets, shifts, step_size, threshold):
    planes, frames_dev, _, width_y, width_z = image.shape
    frames = frames_dev * lax.axis_size("frame")
    cos_y, sin_y = dft_tables(width_y)
    cos_z, sin_z = dft_tables(width_z)
    right_table = jnp.concatenate([cos_z, sin_z], axis=1)
    left_forward = jnp.concatenate(
        [jnp.concatenate([cos_y, sin_y], axis=1), jnp.concatenate([-sin_y, cos_y], axis=1)], axis=0
    )
    left_inverse = jnp.concatenate(
        [jnp.concatenate([cos_y, -sin_y], axis=1), jnp.concatenate([sin_y, cos_y], axis=1)], axis=0
    )
    rows_y = jnp.arange(width_y, dtype=jnp.int32)
    rows_z = jnp.arange(width_z, dtype=jnp.int32)
    low_y = (rows_y < CENTER) | (rows_y >= width_y - CENTER)
    low_z = (rows_z < CENTER) | (rows_z >= width_z - CENTER)
    regular = (rows_z[None, None, :] + offsets[:, :, None]) % ACCEL == 0
    sampled = (regular | low_y[None, :, None] & low_z[None, None, :]).astype(jnp.float32)
    image_re = image[:, :, 0]
    image_im = image[:, :, 1]
    maps = sens.astype(jnp.float32)
    sens_re = maps[:, :, 0][:, :, None]
    sens_im = maps[:, :, 1][:, :, None]
    coil_re = sens_re * image_re[None] - sens_im * image_im[None]
    coil_im = sens_re * image_im[None] + sens_im * image_re[None]
    stacked = jnp.stack([coil_re, coil_im], axis=3)
    spectra = along_y(along_z(stacked, right_table, 1.0, width_z), left_forward)
    resid = sampled[None, None, :, None] * (spectra - kspace.astype(jnp.float32))
    returned = along_z(along_y(resid, left_inverse), right_table, -1.0, width_z)
    back_re = returned[:, :, :, 0]
    back_im = returned[:, :, :, 1]
    grad_re = jnp.sum(sens_re * back_re + sens_im * back_im, axis=0)
    grad_im = jnp.sum(sens_re * back_im - sens_im * back_re, axis=0)
    moved = image - step_size[0] * jnp.stack([grad_re, grad_im], axis=2)
    rolled = jnp.roll(moved, (shifts[0], shifts[1]), axis=(3, 4))
    nyb = width_y // PATCH_Y
    nzb = width_z // PATCH_Z
    voxels = planes * PATCH_Y * PATCH_Z
    blocks = rolled.reshape(planes, frames_dev, 2, nyb, PATCH_Y, nzb, PATCH_Z)
    blocks = blocks.transpose(3, 5, 1, 2, 0, 4, 6).reshape(nyb * nzb, frames_dev, 2, voxels)
    regrouped = lax.all_to_all(blocks, "frame", split_axis=0, concat_axis=1, tiled=True)
    count = regrouped.shape[0]
    casorati = regrouped.reshape(count, 2 * frames, voxels)
    level = threshold[0]
    parity = lax.axis_index("plane") % 2
    halfway = count // 2
    first_part = casorati[:halfway]
    second_part = casorati[halfway:]
    kept_part = jnp.where(parity == 0, first_part, second_part)
    outgoing = jnp.where(parity == 0, second_part, first_part)
    incoming = from_partner(outgoing, "plane", 0)
    complete = jnp.concatenate([kept_part, incoming], axis=2)
    finished = shrink(complete, gram_of(complete), level)
    own_part = finished[:, :, :voxels]
    returned_part = from_partner(finished[:, :, voxels:], "plane", 0)
    shrunk = jnp.where(
        parity == 0,
        jnp.concatenate([own_part, returned_part], axis=0),
        jnp.concatenate([returned_part, own_part], axis=0),
    )
    restored = lax.all_to_all(
        shrunk.reshape(count, frames, 2, voxels), "frame", split_axis=1, concat_axis=0, tiled=True
    )
    placed = restored.reshape(nyb, nzb, frames_dev, 2, planes, PATCH_Y, PATCH_Z)
    placed = placed.transpose(4, 2, 3, 0, 5, 1, 6).reshape(planes, frames_dev, 2, width_y, width_z)
    return jnp.roll(placed, (-shifts[0], -shifts[1]), axis=(3, 4))


VMEM_BYTES = 24 * 1024 * 1024


ZONES = "WYXZ"


def two_parts(table):
    high = table.astype(jnp.bfloat16)
    return high, (table - high.astype(np.float64)).astype(jnp.bfloat16)


def block_tables(length):
    indices = np.arange(length)
    angles = (indices[:, None] * indices[None, :] % length) * (2.0 * np.pi / length)
    cos = np.cos(angles) / np.sqrt(length)
    sin = np.sin(angles) / np.sqrt(length)
    centre = np.concatenate([indices[:CENTER], indices[length - CENTER :]])
    into = np.block([[cos, -sin], [sin, cos]])[:, np.concatenate([centre, length + centre])]
    into_high, into_low = two_parts(into)
    from_high, from_low = two_parts(into.T)
    rest = length - 4 * len(centre)
    into = np.concatenate([into_high, into_low, np.zeros((2 * length, rest), jnp.bfloat16)], axis=1)
    rest = length - 6 * len(centre)
    back = np.concatenate([from_high, from_low, from_high, np.zeros((rest, 2 * length), jnp.bfloat16)], axis=0)
    whole = np.concatenate([*two_parts(cos), *two_parts(sin)], axis=0)
    return np.concatenate([whole, into, back[:, :length], back[:, length:]], axis=0)


def lay_tables(parts_ref, table_ref, width):
    low, top = pl.ds(0, width), pl.ds(width, width)
    for k in range(2):
        cos, sin = parts_ref[pl.ds(k * width, width)], parts_ref[pl.ds((2 + k) * width, width)]
        for table, upper, lower in ((0, sin, -sin), (1, -sin, sin)):
            first, second = pl.ds(2 * k * width, width), pl.ds((2 * k + 1) * width, width)
            table_ref[table, first, low] = cos
            table_ref[table, second, top] = cos
            table_ref[table, first, top] = upper
            table_ref[table, second, low] = lower


def halves(values):
    high = values.astype(jnp.bfloat16)
    return high, (values - high.astype(jnp.float32)).astype(jnp.bfloat16)


def mul(left, right):
    return jnp.dot(left, right, preferred_element_type=jnp.float32)


def from_left(table, values):
    count = table.shape[1]
    value_high, value_low = halves(values)
    first = mul(table, value_high)
    return first[:count] + (first[count:] + mul(table[:count], value_low))


def row_patterns(offsets_ref, width_y, width_z):
    lane = lax.broadcasted_iota(jnp.int32, (width_y, width_z), 1)
    row = lax.broadcasted_iota(jnp.int32, (width_y, width_z), 0)
    offset = jnp.broadcast_to(offsets_ref[...].astype(jnp.float32), (width_z, width_y)).T
    wanted = jnp.where(offset == 0.0, 0.0, ACCEL - offset)
    regular = lax.rem(lane, ACCEL).astype(jnp.float32) == wanted
    low_y = (row < CENTER) | (row >= width_y - CENTER)
    low_z = (lane < CENTER) | (lane >= width_z - CENTER)
    centre = low_y & low_z
    scale = float(ACCEL)
    kept = jnp.where(regular | centre, scale, 0.0).astype(jnp.bfloat16)
    extra = jnp.where(centre & jnp.logical_not(regular), scale, 0.0)
    edge = jnp.concatenate([extra[:CENTER], extra[width_y - CENTER :]], axis=0)
    edge = jnp.where(lane[: 2 * CENTER] < CENTER, edge, pltpu.roll(edge, 2 * CENTER, 1))
    slot = lane[: 2 * CENTER]
    edge = jnp.where(slot < 2 * CENTER, edge, jnp.where(slot < 4 * CENTER, pltpu.roll(edge, 2 * CENTER, 1), 0.0))
    half = jnp.where((offset == 0.0) | (offset == 2.0), 1.0, -1.0)
    real = jnp.where(offset == 0.0, 1.0, jnp.where(offset == 2.0, -1.0, 0.0))
    imag = jnp.where(offset == 1.0, -1.0, jnp.where(offset == 3.0, 1.0, 0.0))
    return kept, edge, half, real, imag


def moved_plane(loads, start_later, p, coils, width, image_ref, sens_ref, kspace_ref, parts_ref, table_ref, step, patterns):
    kept, edge, half, real, imag = patterns
    sides = [range(c, min(c + PAIR, coils)) for c in range(0, coils, PAIR)]
    loads["kspace", p].wait()
    known = []
    for side in sides:
        data = jnp.concatenate(
            [jnp.concatenate([kspace_ref[c, p, 0, k] * kept for k in range(2)], axis=1) for c in side], axis=0
        )
        known.append(mul(data, table_ref[0, : 2 * width]) + mul(data, table_ref[0, 2 * width :]))
    loads["image", p].wait()
    loads["sens", p].wait()
    if p == 0:
        start_later()
    image_re = image_ref[p, 0, 0]
    image_im = image_ref[p, 0, 1]

    def sens(c):
        return sens_ref[c, p, 0].astype(jnp.float32), sens_ref[c, p, 1].astype(jnp.float32)

    lines = []
    for side in sides:
        coil_re, coil_im = [], []
        for c in side:
            sens_re, sens_im = sens(c)
            coil_re.append(sens_re * image_re - sens_im * image_im)
            coil_im.append(sens_re * image_im + sens_im * image_re)
        stacked = jnp.concatenate([jnp.concatenate(coil_re, axis=1), jnp.concatenate(coil_im, axis=1)], axis=0)
        lines.append(from_left(table_ref[0], stacked))
    into = parts_ref[pl.ds(4 * width, 2 * width)]
    out = jnp.concatenate([parts_ref[pl.ds(6 * width, width)], parts_ref[pl.ds(7 * width, width)]], axis=1)
    grad_re = jnp.zeros_like(image_re)
    grad_im = jnp.zeros_like(image_im)
    for side, line, data in zip(sides, lines, known):
        count = len(side)

        def part(k, n):
            return line[k * width : (k + 1) * width, n * width : (n + 1) * width]

        low = jnp.concatenate(
            [
                jnp.concatenate(
                    [jnp.concatenate([part(k, n)[:CENTER], part(k, n)[width - CENTER :]], axis=0) for k in range(2)],
                    axis=1,
                )
                for n in range(count)
            ],
            axis=0,
        )
        weight = jnp.concatenate([edge] * count, axis=0)
        found = mul(jnp.concatenate(halves(low), axis=0), into)
        found = found[: low.shape[0]] + found[low.shape[0] :]
        found = weight * (found + pltpu.roll(found, width - 4 * CENTER, 1))
        found_high = found.astype(jnp.bfloat16).astype(jnp.float32)
        three = found_high + pltpu.roll(found_high, 4 * CENTER, 1) + pltpu.roll(found - found_high, 8 * CENTER, 1)
        added = mul(three.astype(jnp.bfloat16), out)
        resid = ([], [])
        for n in range(count):
            both = []
            for k in range(2):
                both.append(part(k, n) + half * pltpu.roll(part(k, n), width // 2, 1))
            turned = [pltpu.roll(value, width // 4, 1) for value in both]
            sums = [
                both[0] + (real * turned[0] - imag * turned[1]),
                both[1] + (real * turned[1] + imag * turned[0]),
            ]
            for k in range(2):
                value = sums[k] - data[n * width : (n + 1) * width, k * width : (k + 1) * width]
                more = added[2 * CENTER * n : 2 * CENTER * (n + 1), k * width : (k + 1) * width]
                resid[k].append(
                    jnp.concatenate(
                        [
                            value[:CENTER] + more[:CENTER],
                            value[CENTER : width - CENTER],
                            value[width - CENTER :] + more[CENTER:],
                        ],
                        axis=0,
                    )
                )
        back = from_left(table_ref[1], jnp.concatenate([jnp.concatenate(r, axis=1) for r in resid], axis=0))
        for n, c in enumerate(side):
            back_re = back[:width, n * width : (n + 1) * width]
            back_im = back[width:, n * width : (n + 1) * width]
            sens_re, sens_im = sens(c)
            grad_re += sens_re * back_re + sens_im * back_im
            grad_im += sens_re * back_im - sens_im * back_re
    scaled = step * (1.0 / ACCEL)
    return image_re - scaled * grad_re, image_im - scaled * grad_im


def sweep(matrix, order):
    for k in range(order):
        pivot = 1.0 / matrix[k, k][0]
        column = {}
        for i in range(order):
            if i > k:
                column[i] = matrix[i, k]
            elif i < k:
                column[i] = (matrix[k, i][0], -matrix[k, i][1])
        scaled = {i: (re * pivot, im * pivot) for i, (re, im) in column.items()}
        for i in column:
            for j in column:
                if j > i:
                    continue
                a_re, a_im = scaled[i]
                b_re, b_im = column[j]
                re, im = matrix[i, j]
                re = re - (a_re * b_re + a_im * b_im)
                if i != j:
                    im = im - (a_im * b_re - a_re * b_im)
                matrix[i, j] = (re, im)
        for i in column:
            if i > k:
                matrix[i, k] = scaled[i]
            else:
                matrix[k, i] = (scaled[i][0], -scaled[i][1])
        matrix[k, k] = (-pivot, None)
    return matrix


def step_kernel(
    planes, frames, group, coils, width_y, width_z,
    step_ref, level_ref, shifts_hbm, offsets_hbm, image_hbm, sens_hbm, kspace_hbm, table_hbm,
    out_ref,
    shifts_ref, offsets_ref, image_ref, sens_ref, kspace_ref, parts_ref, table_ref, load_sem,
    wrapped, rolled, gathered, entries, inverse, finished, landed,
    send_out, recv_out, send_back, recv_back,
):
    total = frames * group
    plane_me = lax.axis_index("plane")
    frame_me = lax.axis_index("frame")
    part_me = lax.rem(plane_me, group)
    base = plane_me - part_me
    me = frame_me * group + part_me
    rows = PATCH_Y
    everyone = [(f, q) for f in range(frames) for q in range(group)]

    def other(f, q):
        return (frame_me != f) | (part_me != q)

    barrier = pltpu.get_barrier_semaphore()
    for f, q in everyone:

        @pl.when(other(f, q))
        def _():
            pl.semaphore_signal(
                barrier, inc=1, device_id={"plane": base + q, "frame": f}, device_id_type=pl.DeviceIdType.MESH
            )

    loads = {}

    def load(name, source, target):
        loads[name] = pltpu.make_async_copy(source, target, load_sem.at[len(loads)])
        loads[name].start()

    load("offsets", offsets_hbm, offsets_ref)
    load("table", table_hbm, parts_ref)

    def load_plane(p):
        load(("kspace", p), kspace_hbm.at[:, p], kspace_ref.at[:, p])
        load(("image", p), image_hbm.at[p], image_ref.at[p])
        load(("sens", p), sens_hbm.at[:, p], sens_ref.at[:, p])

    load_plane(0)
    load("shifts", shifts_hbm, shifts_ref)

    def start_later():
        for p in range(1, planes):
            load_plane(p)

    loads["offsets"].wait()
    patterns = row_patterns(offsets_ref, width_y, width_z)
    loads["table"].wait()
    lay_tables(parts_ref, table_ref, width_y)

    half, quarter = frames // 2, frames // 4
    inner = lax.rem(frame_me, quarter)

    first, second, third, last = [list(range(b * quarter, (b + 1) * quarter)) for b in range(4)]
    order_home = first[:1] + last[:1] + first[1:] + third[:1] + second + last[1:] + third[1:]

    def order_out(token):
        z_high, z_low = {"W": (0, 0), "X": (0, 1), "Y": (1, 0), "Z": (1, 1)}[token]
        for k in reversed(range(quarter)):
            x = lax.rem(inner + k, quarter)
            for r in reversed(range(group)):
                q = lax.rem(part_me + r, group)
                yield z_high * half + z_low * quarter + x, q, k == 0 and r == 0

    def send(p, f, q, maybe):
        block = rolled.at[p, :, pl.ds(pl.multiple_of((f * group + q) * rows, rows), rows), :]
        copy = pltpu.make_async_remote_copy(
            src_ref=block,
            dst_ref=gathered.at[p, part_me, frame_me],
            send_sem=send_out.at[p],
            recv_sem=recv_out.at[p],
            device_id={"plane": base + q, "frame": f},
            device_id_type=pl.DeviceIdType.MESH,
        )
        if maybe:
            pl.when(other(f, q))(copy.start)
        else:
            copy.start()

    def landed_all(ref, sem):
        pltpu.make_async_copy(ref, ref, sem).wait()

    for p in range(planes):
        moved = moved_plane(loads, start_later, p, coils, width_y, image_ref, sens_ref, kspace_ref, parts_ref, table_ref, step_ref[0], patterns)
        if p == 0:
            loads["shifts"].wait()
        for k in range(2):
            part = pltpu.roll(moved[k], shifts_ref[1], 1)
            wrapped[p, k, pl.ds(0, rows), :] = part[width_y - rows :]
            wrapped[p, k, pl.ds(rows, width_y), :] = part
            rolled[p, k] = wrapped[p, k, pl.ds(rows - shifts_ref[0], width_y), :]
        if p == 0:
            pl.semaphore_wait(barrier, total - 1)
        pltpu.make_async_copy(
            rolled.at[p, :, pl.ds(pl.multiple_of(me * rows, rows), rows), :],
            gathered.at[p, part_me, frame_me],
            recv_out.at[p],
        ).start()
        for zone in ZONES:
            for f, q, maybe in order_out(zone):
                send(p, f, q, maybe)

    pairs = [(f, g) for f in range(frames) for g in range(f + 1)]
    for p in range(planes):
        landed_all(gathered.at[p], recv_out.at[p])
        for n, (f, g) in enumerate(pairs):
            sum_re = None
            sum_im = None
            for q in range(group):
                f_re, f_im = gathered[p, q, f, 0], gathered[p, q, f, 1]
                g_re, g_im = gathered[p, q, g, 0], gathered[p, q, g, 1]
                re = f_re * g_re + f_im * g_im
                sum_re = re if sum_re is None else sum_re + re
                if f != g:
                    im = f_im * g_re - f_re * g_im
                    sum_im = im if sum_im is None else sum_im + im
            spot = f * frames + g
            entries[spot] = sum_re if p == 0 else entries[spot] + sum_re
            if f != g:
                spot = g * frames + f
                entries[spot] = sum_im if p == 0 else entries[spot] + sum_im

    one_row = lax.broadcasted_iota(jnp.int32, (width_z, width_z), 0) // PATCH_Z
    one_lane = lax.broadcasted_iota(jnp.int32, (width_z, width_z), 1) // PATCH_Z
    same = (one_row == one_lane).astype(jnp.bfloat16)
    cells = entries[...]
    shift = rows // 2
    while shift:
        cells = cells + pltpu.roll(cells, shift, 1)
        shift //= 2
    high, low = halves(cells.reshape(frames * frames * rows, width_z))
    entries[...] = (mul(high, same) + mul(low, same)).reshape(frames * frames, rows, width_z)

    level = level_ref[0]
    matrix = {}
    for f, g in pairs:
        if f == g:
            matrix[f, f] = (entries[f * frames + f] + level, None)
        else:
            matrix[f, g] = (entries[f * frames + g], entries[g * frames + f])
    matrix = sweep(matrix, frames)
    for f, g in pairs:
        re, im = matrix[f, g]
        inverse[f, g, 0] = re * level
        if f != g:
            inverse[f, g, 1] = im * level
            inverse[g, f, 0] = re * level
            inverse[g, f, 1] = -im * level
        else:
            inverse[f, f, 1] = jnp.zeros_like(re)

    spot = pl.ds(pl.multiple_of(me * rows, rows), rows)
    for f in order_home:
        weights = [(inverse[f, g, 0], inverse[f, g, 1]) for g in range(frames)]
        for q in range(group):
            for p in range(planes):
                re = gathered[p, q, f, 0]
                im = gathered[p, q, f, 1]
                for g in range(frames):
                    g_re, g_im = gathered[p, q, g, 0], gathered[p, q, g, 1]
                    w_re, w_im = weights[g]
                    re = re + (w_re * g_re - w_im * g_im)
                    im = im + (w_re * g_im + w_im * g_re)
                finished[q, f, p, 0] = re
                finished[q, f, p, 1] = im
            place = landed.at[:, :, spot, :]
            apart = other(f, q)
            copy = pltpu.make_async_remote_copy(
                src_ref=finished.at[q, f],
                dst_ref=place,
                send_sem=send_back,
                recv_sem=recv_back,
                device_id={"plane": base + q, "frame": f},
                device_id_type=pl.DeviceIdType.MESH,
            )
            pl.when(apart)(copy.start)
            pl.when(jnp.logical_not(apart))(pltpu.make_async_copy(finished.at[q, f], place, recv_back).start)
    sent = pl.ds(0, (total - 1) * rows)
    for p in range(planes):
        landed_all(rolled.at[p, :, sent, :], send_out.at[p])
    landed_all(landed, recv_back)
    shift_z = lax.rem(width_z - shifts_ref[1], width_z)
    for p in range(planes):
        for k in range(2):
            part = pltpu.roll(landed[p, k], shift_z, 1)
            wrapped[p, k, pl.ds(0, width_y), :] = part
            wrapped[p, k, pl.ds(width_y, rows), :] = part[:rows]
            out_ref[p, 0, k] = wrapped[p, k, pl.ds(shifts_ref[0], width_y), :]
    landed_all(landed.at[:, :, sent, :], send_back)


def local_fused(image, sens, kspace, offsets, shifts, step_size, threshold):
    planes, _, _, width_y, width_z = image.shape
    coils = sens.shape[0]
    frames = lax.axis_size("frame")
    group = PATCH_X // planes
    total = frames * group
    table = jnp.asarray(block_tables(width_y))
    vmem = pl.BlockSpec(memory_space=pltpu.VMEM)
    smem = pl.BlockSpec(memory_space=pltpu.SMEM)
    hbm = pl.BlockSpec(memory_space=pltpu.HBM)
    slab = (PATCH_Y, width_z)
    dma = pltpu.SemaphoreType.DMA
    in_hbm = [
        pltpu.with_memory_space_constraint(x, pltpu.HBM) for x in (shifts, offsets, image, sens, kspace, table)
    ]
    return pl.pallas_call(
        functools.partial(step_kernel, planes, frames, group, coils, width_y, width_z),
        out_shape=jax.ShapeDtypeStruct(image.shape, jnp.float32),
        in_specs=[smem, smem] + [hbm] * 6,
        out_specs=vmem,
        scratch_shapes=[
            pltpu.SMEM(shifts.shape, shifts.dtype),
            pltpu.VMEM(offsets.shape, offsets.dtype),
            pltpu.VMEM(image.shape, image.dtype),
            pltpu.VMEM(sens.shape, sens.dtype),
            pltpu.VMEM(kspace.shape, kspace.dtype),
            pltpu.VMEM(table.shape, table.dtype),
            pltpu.VMEM((2, 4 * width_y, 2 * width_y), table.dtype),
            dma((3 * planes + 3,)),
            pltpu.VMEM((planes, 2, width_y + PATCH_Y, width_z), jnp.float32),
            pltpu.VMEM((planes, 2, width_y, width_z), jnp.float32),
            pltpu.VMEM((planes, group, frames, 2) + slab, jnp.float32),
            pltpu.VMEM((frames * frames,) + slab, jnp.float32),
            pltpu.VMEM((frames, frames, 2) + slab, jnp.float32),
            pltpu.VMEM((group, frames, planes, 2) + slab, jnp.float32),
            pltpu.VMEM((planes, 2, width_y, width_z), jnp.float32),
            dma((planes,)),
            dma((planes,)),
            dma(()),
            dma(()),
        ],
        compiler_params=pltpu.CompilerParams(collective_id=0, has_side_effects=True, vmem_limit_bytes=VMEM_BYTES),
        name="prox_step",
    )(step_size, threshold, *in_hbm)


def local(image, sens, kspace, offsets, shifts, step_size, threshold):
    planes, frames_dev, _, width_y, width_z = image.shape
    frames = frames_dev * lax.axis_size("frame")
    group = PATCH_X // planes
    one_block = frames * group * PATCH_Y == width_y and frames_dev == 1 and frames & (frames - 1) == 0 and frames >= 4
    split = group > 1 and group & (group - 1) == 0 and lax.axis_size("plane") % group == 0
    if one_block and split and width_y == width_z and width_z % 128 == 0:
        return local_fused(image, sens, kspace, offsets, shifts, step_size, threshold)
    return local_general(image, sens, kspace, offsets, shifts, step_size, threshold)


def solution(mesh):
    in_specs = (
        P("plane", "frame", None, None, None),
        P(None, "plane", None, None, None),
        P(None, "plane", "frame", None, None, None),
        P("frame", None),
        P(),
        P(),
        P(),
    )
    out_specs = P("plane", "frame", None, None, None)
    return jax.shard_map(local, mesh=mesh, in_specs=in_specs, out_specs=out_specs, check_vma=False)
```

```python
import functools
import math

import jax
import jax.numpy as jnp
import numpy as np
from jax import lax
from jax.experimental import pallas as pl
from jax.experimental.pallas import tpu as pltpu
from jax.sharding import PartitionSpec as P

PATCH_X = 4
PATCH_Y = 8
PATCH_Z = 8
ACCEL = 4
CENTER = 8
PAIR = 2


def from_partner(block, axis, distance):
    count = lax.axis_size(axis)
    route = []
    for low in range(count):
        high = low | 1 << distance
        if high != low and high < count:
            route += [(low, high), (high, low)]
    return lax.ppermute(block, axis, route)


def dft_tables(length):
    indices = jnp.arange(length, dtype=jnp.int32)
    phases = indices[:, None] * indices[None, :] % length
    angles = phases.astype(jnp.float32) * (2.0 * math.pi / length)
    norm_scale = 1.0 / math.sqrt(length)
    return (jnp.cos(angles) * norm_scale, jnp.sin(angles) * norm_scale)


def along_z(stacked, right_table, sign, width_z):
    product = jnp.einsum(
        "...z,zw->...w",
        stacked,
        right_table,
        precision=lax.Precision.HIGHEST,
        preferred_element_type=jnp.float32,
    )
    cos_part = product[..., :width_z]
    sin_part = product[..., width_z:]
    real_part = cos_part[..., 0, :, :] + sign * sin_part[..., 1, :, :]
    imag_part = cos_part[..., 1, :, :] - sign * sin_part[..., 0, :, :]
    return jnp.stack([real_part, imag_part], axis=-3)


def along_y(stacked, left_table):
    shape_in = stacked.shape
    merged = stacked.reshape(shape_in[:-3] + (2 * shape_in[-2], shape_in[-1]))
    result = jnp.einsum(
        "ur,...rz->...uz",
        left_table,
        merged,
        precision=lax.Precision.HIGHEST,
        preferred_element_type=jnp.float32,
    )
    return result.reshape(shape_in)


def rotate(casorati):
    frames2, voxels = (casorati.shape[-2], casorati.shape[-1])
    split_parts = casorati.reshape(casorati.shape[:-2] + (frames2 // 2, 2, voxels))
    turned = jnp.stack([-split_parts[..., 1, :], split_parts[..., 0, :]], axis=-2)
    return turned.reshape(casorati.shape)


def gram_of(casorati):
    twin = rotate(casorati)
    first = jnp.einsum(
        "kav,kbv->kab",
        casorati,
        casorati,
        precision=lax.Precision.HIGHEST,
        preferred_element_type=jnp.float32,
    )
    second = jnp.einsum(
        "kav,kbv->kab",
        twin,
        twin,
        precision=lax.Precision.HIGHEST,
        preferred_element_type=jnp.float32,
    )
    return first + second


def shrink(casorati, gram, level):
    order = gram.shape[-1]
    system = gram + level * jnp.eye(order, dtype=jnp.float32)
    factor = jnp.linalg.cholesky(system)
    forward_part = jax.scipy.linalg.solve_triangular(factor, casorati, lower=True)
    solved = jax.scipy.linalg.solve_triangular(factor, forward_part, lower=True, trans=1)
    return casorati - level * solved


def local_general(image, sens, kspace, offsets, shifts, step_size, threshold):
    planes, frames_dev, _, width_y, width_z = image.shape
    frames = frames_dev * lax.axis_size("frame")
    cos_y, sin_y = dft_tables(width_y)
    cos_z, sin_z = dft_tables(width_z)
    right_table = jnp.concatenate([cos_z, sin_z], axis=1)
    left_forward = jnp.concatenate(
        [jnp.concatenate([cos_y, sin_y], axis=1), jnp.concatenate([-sin_y, cos_y], axis=1)], axis=0
    )
    left_inverse = jnp.concatenate(
        [jnp.concatenate([cos_y, -sin_y], axis=1), jnp.concatenate([sin_y, cos_y], axis=1)], axis=0
    )
    rows_y = jnp.arange(width_y, dtype=jnp.int32)
    rows_z = jnp.arange(width_z, dtype=jnp.int32)
    low_y = (rows_y < CENTER) | (rows_y >= width_y - CENTER)
    low_z = (rows_z < CENTER) | (rows_z >= width_z - CENTER)
    regular = (rows_z[None, None, :] + offsets[:, :, None]) % ACCEL == 0
    sampled = (regular | low_y[None, :, None] & low_z[None, None, :]).astype(jnp.float32)
    image_re = image[:, :, 0]
    image_im = image[:, :, 1]
    maps = sens.astype(jnp.float32)
    sens_re = maps[:, :, 0][:, :, None]
    sens_im = maps[:, :, 1][:, :, None]
    coil_re = sens_re * image_re[None] - sens_im * image_im[None]
    coil_im = sens_re * image_im[None] + sens_im * image_re[None]
    stacked = jnp.stack([coil_re, coil_im], axis=3)
    spectra = along_y(along_z(stacked, right_table, 1.0, width_z), left_forward)
    resid = sampled[None, None, :, None] * (spectra - kspace.astype(jnp.float32))
    returned = along_z(along_y(resid, left_inverse), right_table, -1.0, width_z)
    back_re = returned[:, :, :, 0]
    back_im = returned[:, :, :, 1]
    grad_re = jnp.sum(sens_re * back_re + sens_im * back_im, axis=0)
    grad_im = jnp.sum(sens_re * back_im - sens_im * back_re, axis=0)
    moved = image - step_size[0] * jnp.stack([grad_re, grad_im], axis=2)
    rolled = jnp.roll(moved, (shifts[0], shifts[1]), axis=(3, 4))
    nyb = width_y // PATCH_Y
    nzb = width_z // PATCH_Z
    voxels = planes * PATCH_Y * PATCH_Z
    blocks = rolled.reshape(planes, frames_dev, 2, nyb, PATCH_Y, nzb, PATCH_Z)
    blocks = blocks.transpose(3, 5, 1, 2, 0, 4, 6).reshape(nyb * nzb, frames_dev, 2, voxels)
    regrouped = lax.all_to_all(blocks, "frame", split_axis=0, concat_axis=1, tiled=True)
    count = regrouped.shape[0]
    casorati = regrouped.reshape(count, 2 * frames, voxels)
    level = threshold[0]
    parity = lax.axis_index("plane") % 2
    halfway = count // 2
    first_part = casorati[:halfway]
    second_part = casorati[halfway:]
    kept_part = jnp.where(parity == 0, first_part, second_part)
    outgoing = jnp.where(parity == 0, second_part, first_part)
    incoming = from_partner(outgoing, "plane", 0)
    complete = jnp.concatenate([kept_part, incoming], axis=2)
    finished = shrink(complete, gram_of(complete), level)
    own_part = finished[:, :, :voxels]
    returned_part = from_partner(finished[:, :, voxels:], "plane", 0)
    shrunk = jnp.where(
        parity == 0,
        jnp.concatenate([own_part, returned_part], axis=0),
        jnp.concatenate([returned_part, own_part], axis=0),
    )
    restored = lax.all_to_all(
        shrunk.reshape(count, frames, 2, voxels), "frame", split_axis=1, concat_axis=0, tiled=True
    )
    placed = restored.reshape(nyb, nzb, frames_dev, 2, planes, PATCH_Y, PATCH_Z)
    placed = placed.transpose(4, 2, 3, 0, 5, 1, 6).reshape(planes, frames_dev, 2, width_y, width_z)
    return jnp.roll(placed, (-shifts[0], -shifts[1]), axis=(3, 4))


VMEM_BYTES = 24 * 1024 * 1024


ZONES = "WYXZ"


def two_parts(table):
    high = table.astype(jnp.bfloat16)
    return high, (table - high.astype(np.float64)).astype(jnp.bfloat16)


def block_tables(length):
    indices = np.arange(length)
    angles = (indices[:, None] * indices[None, :] % length) * (2.0 * np.pi / length)
    cos = np.cos(angles) / np.sqrt(length)
    sin = np.sin(angles) / np.sqrt(length)
    centre = np.concatenate([indices[:CENTER], indices[length - CENTER :]])
    into = np.block([[cos, -sin], [sin, cos]])[:, np.concatenate([centre, length + centre])]
    into_high, into_low = two_parts(into)
    from_high, from_low = two_parts(into.T)
    rest = length - 4 * len(centre)
    into = np.concatenate([into_high, into_low, np.zeros((2 * length, rest), jnp.bfloat16)], axis=1)
    rest = length - 6 * len(centre)
    back = np.concatenate([from_high, from_low, from_high, np.zeros((rest, 2 * length), jnp.bfloat16)], axis=0)
    whole = np.concatenate([*two_parts(cos), *two_parts(sin)], axis=0)
    return np.concatenate([whole, into, back[:, :length], back[:, length:]], axis=0)


def lay_tables(parts_ref, table_ref, width):
    low, top = pl.ds(0, width), pl.ds(width, width)
    for k in range(2):
        cos, sin = parts_ref[pl.ds(k * width, width)], parts_ref[pl.ds((2 + k) * width, width)]
        for table, upper, lower in ((0, sin, -sin), (1, -sin, sin)):
            first, second = pl.ds(2 * k * width, width), pl.ds((2 * k + 1) * width, width)
            table_ref[table, first, low] = cos
            table_ref[table, second, top] = cos
            table_ref[table, first, top] = upper
            table_ref[table, second, low] = lower


def halves(values):
    high = values.astype(jnp.bfloat16)
    return high, (values - high.astype(jnp.float32)).astype(jnp.bfloat16)


def mul(left, right):
    return jnp.dot(left, right, preferred_element_type=jnp.float32)


def from_left(table, values):
    count = table.shape[1]
    value_high, value_low = halves(values)
    first = mul(table, value_high)
    return first[:count] + (first[count:] + mul(table[:count], value_low))


def row_patterns(offsets_ref, width_y, width_z):
    lane = lax.broadcasted_iota(jnp.int32, (width_y, width_z), 1)
    row = lax.broadcasted_iota(jnp.int32, (width_y, width_z), 0)
    offset = jnp.broadcast_to(offsets_ref[...].astype(jnp.float32), (width_z, width_y)).T
    wanted = jnp.where(offset == 0.0, 0.0, ACCEL - offset)
    regular = lax.rem(lane, ACCEL).astype(jnp.float32) == wanted
    low_y = (row < CENTER) | (row >= width_y - CENTER)
    low_z = (lane < CENTER) | (lane >= width_z - CENTER)
    centre = low_y & low_z
    scale = float(ACCEL)
    kept = jnp.where(regular | centre, scale, 0.0).astype(jnp.bfloat16)
    extra = jnp.where(centre & jnp.logical_not(regular), scale, 0.0)
    edge = jnp.concatenate([extra[:CENTER], extra[width_y - CENTER :]], axis=0)
    edge = jnp.where(lane[: 2 * CENTER] < CENTER, edge, pltpu.roll(edge, 2 * CENTER, 1))
    slot = lane[: 2 * CENTER]
    edge = jnp.where(slot < 2 * CENTER, edge, jnp.where(slot < 4 * CENTER, pltpu.roll(edge, 2 * CENTER, 1), 0.0))
    half = jnp.where((offset == 0.0) | (offset == 2.0), 1.0, -1.0)
    real = jnp.where(offset == 0.0, 1.0, jnp.where(offset == 2.0, -1.0, 0.0))
    imag = jnp.where(offset == 1.0, -1.0, jnp.where(offset == 3.0, 1.0, 0.0))
    return kept, edge, half, real, imag


def moved_plane(loads, start_later, p, coils, width, image_ref, sens_ref, kspace_ref, parts_ref, table_ref, step, patterns):
    kept, edge, half, real, imag = patterns
    sides = [range(c, min(c + PAIR, coils)) for c in range(0, coils, PAIR)]
    loads["kspace", p].wait()
    known = []
    for side in sides:
        data = jnp.concatenate(
            [jnp.concatenate([kspace_ref[c, p, 0, k] * kept for k in range(2)], axis=1) for c in side], axis=0
        )
        known.append(mul(data, table_ref[0, : 2 * width]) + mul(data, table_ref[0, 2 * width :]))
    loads["image", p].wait()
    loads["sens", p].wait()
    if p == 0:
        start_later()
    image_re = image_ref[p, 0, 0]
    image_im = image_ref[p, 0, 1]

    def sens(c):
        return sens_ref[c, p, 0].astype(jnp.float32), sens_ref[c, p, 1].astype(jnp.float32)

    lines = []
    for side in sides:
        coil_re, coil_im = [], []
        for c in side:
            sens_re, sens_im = sens(c)
            coil_re.append(sens_re * image_re - sens_im * image_im)
            coil_im.append(sens_re * image_im + sens_im * image_re)
        stacked = jnp.concatenate([jnp.concatenate(coil_re, axis=1), jnp.concatenate(coil_im, axis=1)], axis=0)
        lines.append(from_left(table_ref[0], stacked))
    into = parts_ref[pl.ds(4 * width, 2 * width)]
    out = jnp.concatenate([parts_ref[pl.ds(6 * width, width)], parts_ref[pl.ds(7 * width, width)]], axis=1)
    grad_re = jnp.zeros_like(image_re)
    grad_im = jnp.zeros_like(image_im)
    for side, line, data in zip(sides, lines, known):
        count = len(side)

        def part(k, n):
            return line[k * width : (k + 1) * width, n * width : (n + 1) * width]

        low = jnp.concatenate(
            [
                jnp.concatenate(
                    [jnp.concatenate([part(k, n)[:CENTER], part(k, n)[width - CENTER :]], axis=0) for k in range(2)],
                    axis=1,
                )
                for n in range(count)
            ],
            axis=0,
        )
        weight = jnp.concatenate([edge] * count, axis=0)
        found = mul(jnp.concatenate(halves(low), axis=0), into)
        found = found[: low.shape[0]] + found[low.shape[0] :]
        found = weight * (found + pltpu.roll(found, width - 4 * CENTER, 1))
        found_high = found.astype(jnp.bfloat16).astype(jnp.float32)
        three = found_high + pltpu.roll(found_high, 4 * CENTER, 1) + pltpu.roll(found - found_high, 8 * CENTER, 1)
        added = mul(three.astype(jnp.bfloat16), out)
        resid = ([], [])
        for n in range(count):
            both = []
            for k in range(2):
                both.append(part(k, n) + half * pltpu.roll(part(k, n), width // 2, 1))
            turned = [pltpu.roll(value, width // 4, 1) for value in both]
            sums = [
                both[0] + (real * turned[0] - imag * turned[1]),
                both[1] + (real * turned[1] + imag * turned[0]),
            ]
            for k in range(2):
                value = sums[k] - data[n * width : (n + 1) * width, k * width : (k + 1) * width]
                more = added[2 * CENTER * n : 2 * CENTER * (n + 1), k * width : (k + 1) * width]
                resid[k].append(
                    jnp.concatenate(
                        [
                            value[:CENTER] + more[:CENTER],
                            value[CENTER : width - CENTER],
                            value[width - CENTER :] + more[CENTER:],
                        ],
                        axis=0,
                    )
                )
        back = from_left(table_ref[1], jnp.concatenate([jnp.concatenate(r, axis=1) for r in resid], axis=0))
        for n, c in enumerate(side):
            back_re = back[:width, n * width : (n + 1) * width]
            back_im = back[width:, n * width : (n + 1) * width]
            sens_re, sens_im = sens(c)
            grad_re += sens_re * back_re + sens_im * back_im
            grad_im += sens_re * back_im - sens_im * back_re
    scaled = step * (1.0 / ACCEL)
    return image_re - scaled * grad_re, image_im - scaled * grad_im


def sweep(matrix, order):
    for k in range(order):
        pivot = 1.0 / matrix[k, k][0]
        column = {}
        for i in range(order):
            if i > k:
                column[i] = matrix[i, k]
            elif i < k:
                column[i] = (matrix[k, i][0], -matrix[k, i][1])
        scaled = {i: (re * pivot, im * pivot) for i, (re, im) in column.items()}
        for i in column:
            for j in column:
                if j > i:
                    continue
                a_re, a_im = scaled[i]
                b_re, b_im = column[j]
                re, im = matrix[i, j]
                re = re - (a_re * b_re + a_im * b_im)
                if i != j:
                    im = im - (a_im * b_re - a_re * b_im)
                matrix[i, j] = (re, im)
        for i in column:
            if i > k:
                matrix[i, k] = scaled[i]
            else:
                matrix[k, i] = (scaled[i][0], -scaled[i][1])
        matrix[k, k] = (-pivot, None)
    return matrix


def step_kernel(
    planes, frames, group, coils, width_y, width_z,
    step_ref, level_ref, shifts_hbm, offsets_hbm, image_hbm, sens_hbm, kspace_hbm, table_hbm,
    out_ref,
    shifts_ref, offsets_ref, image_ref, sens_ref, kspace_ref, parts_ref, table_ref, load_sem,
    wrapped, rolled, gathered, entries, inverse, finished, landed,
    send_out, recv_out, send_back, recv_back,
):
    total = frames * group
    plane_me = lax.axis_index("plane")
    frame_me = lax.axis_index("frame")
    part_me = lax.rem(plane_me, group)
    base = plane_me - part_me
    me = frame_me * group + part_me
    rows = PATCH_Y
    everyone = [(f, q) for f in range(frames) for q in range(group)]

    def other(f, q):
        return (frame_me != f) | (part_me != q)

    loads = {}

    def load(name, source, target):
        loads[name] = pltpu.make_async_copy(source, target, load_sem.at[len(loads)])
        loads[name].start()

    load("offsets", offsets_hbm, offsets_ref)
    load("table", table_hbm, parts_ref)

    def load_plane(p):
        load(("kspace", p), kspace_hbm.at[:, p], kspace_ref.at[:, p])
        load(("image", p), image_hbm.at[p], image_ref.at[p])
        load(("sens", p), sens_hbm.at[:, p], sens_ref.at[:, p])

    load_plane(0)
    load("shifts", shifts_hbm, shifts_ref)

    barrier = pltpu.get_barrier_semaphore()
    for f, q in everyone:

        @pl.when(other(f, q))
        def _():
            pl.semaphore_signal(
                barrier, inc=1, device_id={"plane": base + q, "frame": f}, device_id_type=pl.DeviceIdType.MESH
            )

    def start_later():
        for p in range(1, planes):
            load_plane(p)

    loads["offsets"].wait()
    patterns = row_patterns(offsets_ref, width_y, width_z)
    loads["table"].wait()
    lay_tables(parts_ref, table_ref, width_y)

    half, quarter = frames // 2, frames // 4
    inner = lax.rem(frame_me, quarter)

    first, second, third, last = [list(range(b * quarter, (b + 1) * quarter)) for b in range(4)]
    order_home = first[:1] + last[:1] + first[1:] + third[:1] + second + last[1:] + third[1:]

    def order_out(token):
        z_high, z_low = {"W": (0, 0), "X": (0, 1), "Y": (1, 0), "Z": (1, 1)}[token]
        for k in reversed(range(quarter)):
            x = lax.rem(inner + k, quarter)
            for r in reversed(range(group)):
                q = lax.rem(part_me + r, group)
                yield z_high * half + z_low * quarter + x, q, k == 0 and r == 0

    def send(p, f, q, maybe):
        block = rolled.at[p, :, pl.ds(pl.multiple_of((f * group + q) * rows, rows), rows), :]
        copy = pltpu.make_async_remote_copy(
            src_ref=block,
            dst_ref=gathered.at[p, part_me, frame_me],
            send_sem=send_out.at[p],
            recv_sem=recv_out.at[p],
            device_id={"plane": base + q, "frame": f},
            device_id_type=pl.DeviceIdType.MESH,
        )
        if maybe:
            pl.when(other(f, q))(copy.start)
        else:
            copy.start()

    def landed_all(ref, sem):
        pltpu.make_async_copy(ref, ref, sem).wait()

    for p in range(planes):
        moved = moved_plane(loads, start_later, p, coils, width_y, image_ref, sens_ref, kspace_ref, parts_ref, table_ref, step_ref[0], patterns)
        if p == 0:
            loads["shifts"].wait()
        for k in range(2):
            part = pltpu.roll(moved[k], shifts_ref[1], 1)
            wrapped[p, k, pl.ds(0, rows), :] = part[width_y - rows :]
            wrapped[p, k, pl.ds(rows, width_y), :] = part
            rolled[p, k] = wrapped[p, k, pl.ds(rows - shifts_ref[0], width_y), :]
        if p == 0:
            pl.semaphore_wait(barrier, total - 1)
        pltpu.make_async_copy(
            rolled.at[p, :, pl.ds(pl.multiple_of(me * rows, rows), rows), :],
            gathered.at[p, part_me, frame_me],
            recv_out.at[p],
        ).start()
        for zone in ZONES:
            for f, q, maybe in order_out(zone):
                send(p, f, q, maybe)

    pairs = [(f, g) for f in range(frames) for g in range(f + 1)]
    for p in range(planes):
        landed_all(gathered.at[p], recv_out.at[p])
        for n, (f, g) in enumerate(pairs):
            sum_re = None
            sum_im = None
            for q in range(group):
                f_re, f_im = gathered[p, q, f, 0], gathered[p, q, f, 1]
                g_re, g_im = gathered[p, q, g, 0], gathered[p, q, g, 1]
                re = f_re * g_re + f_im * g_im
                sum_re = re if sum_re is None else sum_re + re
                if f != g:
                    im = f_im * g_re - f_re * g_im
                    sum_im = im if sum_im is None else sum_im + im
            spot = f * frames + g
            entries[spot] = sum_re if p == 0 else entries[spot] + sum_re
            if f != g:
                spot = g * frames + f
                entries[spot] = sum_im if p == 0 else entries[spot] + sum_im

    one_row = lax.broadcasted_iota(jnp.int32, (width_z, width_z), 0) // PATCH_Z
    one_lane = lax.broadcasted_iota(jnp.int32, (width_z, width_z), 1) // PATCH_Z
    same = (one_row == one_lane).astype(jnp.bfloat16)
    cells = entries[...]
    shift = rows // 2
    while shift:
        cells = cells + pltpu.roll(cells, shift, 1)
        shift //= 2
    high, low = halves(cells.reshape(frames * frames * rows, width_z))
    entries[...] = (mul(high, same) + mul(low, same)).reshape(frames * frames, rows, width_z)

    level = level_ref[0]
    matrix = {}
    for f, g in pairs:
        if f == g:
            matrix[f, f] = (entries[f * frames + f] + level, None)
        else:
            matrix[f, g] = (entries[f * frames + g], entries[g * frames + f])
    matrix = sweep(matrix, frames)
    for f, g in pairs:
        re, im = matrix[f, g]
        inverse[f, g, 0] = re * level
        if f != g:
            inverse[f, g, 1] = im * level
            inverse[g, f, 0] = re * level
            inverse[g, f, 1] = -im * level
        else:
            inverse[f, f, 1] = jnp.zeros_like(re)

    spot = pl.ds(pl.multiple_of(me * rows, rows), rows)
    for f in order_home:
        weights = [(inverse[f, g, 0], inverse[f, g, 1]) for g in range(frames)]
        for q in range(group):
            for p in range(planes):
                re = gathered[p, q, f, 0]
                im = gathered[p, q, f, 1]
                for g in range(frames):
                    g_re, g_im = gathered[p, q, g, 0], gathered[p, q, g, 1]
                    w_re, w_im = weights[g]
                    re = re + (w_re * g_re - w_im * g_im)
                    im = im + (w_re * g_im + w_im * g_re)
                finished[q, f, p, 0] = re
                finished[q, f, p, 1] = im
            place = landed.at[:, :, spot, :]
            apart = other(f, q)
            copy = pltpu.make_async_remote_copy(
                src_ref=finished.at[q, f],
                dst_ref=place,
                send_sem=send_back,
                recv_sem=recv_back,
                device_id={"plane": base + q, "frame": f},
                device_id_type=pl.DeviceIdType.MESH,
            )
            pl.when(apart)(copy.start)
            pl.when(jnp.logical_not(apart))(pltpu.make_async_copy(finished.at[q, f], place, recv_back).start)
    sent = pl.ds(0, (total - 1) * rows)
    for p in range(planes):
        landed_all(rolled.at[p, :, sent, :], send_out.at[p])
    landed_all(landed, recv_back)
    shift_z = lax.rem(width_z - shifts_ref[1], width_z)
    for p in range(planes):
        for k in range(2):
            part = pltpu.roll(landed[p, k], shift_z, 1)
            wrapped[p, k, pl.ds(0, width_y), :] = part
            wrapped[p, k, pl.ds(width_y, rows), :] = part[:rows]
            out_ref[p, 0, k] = wrapped[p, k, pl.ds(shifts_ref[0], width_y), :]
    landed_all(landed.at[:, :, sent, :], send_back)


def local_fused(image, sens, kspace, offsets, shifts, step_size, threshold):
    planes, _, _, width_y, width_z = image.shape
    coils = sens.shape[0]
    frames = lax.axis_size("frame")
    group = PATCH_X // planes
    total = frames * group
    table = jnp.asarray(block_tables(width_y))
    vmem = pl.BlockSpec(memory_space=pltpu.VMEM)
    smem = pl.BlockSpec(memory_space=pltpu.SMEM)
    hbm = pl.BlockSpec(memory_space=pltpu.HBM)
    slab = (PATCH_Y, width_z)
    dma = pltpu.SemaphoreType.DMA
    in_hbm = [
        pltpu.with_memory_space_constraint(x, pltpu.HBM) for x in (shifts, offsets, image, sens, kspace, table)
    ]
    return pl.pallas_call(
        functools.partial(step_kernel, planes, frames, group, coils, width_y, width_z),
        out_shape=jax.ShapeDtypeStruct(image.shape, jnp.float32),
        in_specs=[smem, smem] + [hbm] * 6,
        out_specs=vmem,
        scratch_shapes=[
            pltpu.SMEM(shifts.shape, shifts.dtype),
            pltpu.VMEM(offsets.shape, offsets.dtype),
            pltpu.VMEM(image.shape, image.dtype),
            pltpu.VMEM(sens.shape, sens.dtype),
            pltpu.VMEM(kspace.shape, kspace.dtype),
            pltpu.VMEM(table.shape, table.dtype),
            pltpu.VMEM((2, 4 * width_y, 2 * width_y), table.dtype),
            dma((3 * planes + 3,)),
            pltpu.VMEM((planes, 2, width_y + PATCH_Y, width_z), jnp.float32),
            pltpu.VMEM((planes, 2, width_y, width_z), jnp.float32),
            pltpu.VMEM((planes, group, frames, 2) + slab, jnp.float32),
            pltpu.VMEM((frames * frames,) + slab, jnp.float32),
            pltpu.VMEM((frames, frames, 2) + slab, jnp.float32),
            pltpu.VMEM((group, frames, planes, 2) + slab, jnp.float32),
            pltpu.VMEM((planes, 2, width_y, width_z), jnp.float32),
            dma((planes,)),
            dma((planes,)),
            dma(()),
            dma(()),
        ],
        compiler_params=pltpu.CompilerParams(collective_id=0, has_side_effects=True, vmem_limit_bytes=VMEM_BYTES),
        name="prox_step",
    )(step_size, threshold, *in_hbm)


def local(image, sens, kspace, offsets, shifts, step_size, threshold):
    planes, frames_dev, _, width_y, width_z = image.shape
    frames = frames_dev * lax.axis_size("frame")
    group = PATCH_X // planes
    one_block = frames * group * PATCH_Y == width_y and frames_dev == 1 and frames & (frames - 1) == 0 and frames >= 4
    split = group > 1 and group & (group - 1) == 0 and lax.axis_size("plane") % group == 0
    if one_block and split and width_y == width_z and width_z % 128 == 0:
        return local_fused(image, sens, kspace, offsets, shifts, step_size, threshold)
    return local_general(image, sens, kspace, offsets, shifts, step_size, threshold)


def solution(mesh):
    in_specs = (
        P("plane", "frame", None, None, None),
        P(None, "plane", None, None, None),
        P(None, "plane", "frame", None, None, None),
        P("frame", None),
        P(),
        P(),
        P(),
    )
    out_specs = P("plane", "frame", None, None, None)
    return jax.shard_map(local, mesh=mesh, in_specs=in_specs, out_specs=out_specs, check_vma=False)
```
